512 devices in a mesh: gx: 16 (over z), gy: 32 (over y, x, core).
Axes of the slice: x: 4, y: 4, z: 16, core: 2. Of those that a mesh axis runs over, the one named last changes fastest.
Arguments:
- positions: float32 [2, 8388608], P(None, ('gx', 'gy')), may hold values from 0 to 4
- displacement: float32 [2, 8388608], P(None, ('gx', 'gy')), may hold values from -6 to 6
- velocity: float32 [2, 8388608], P(None, ('gx', 'gy')), may hold values from -6 to 6
- stiffness: float32 [8388608], P(('gx', 'gy')), may hold values from 0.5 to 4
- density: float32 [8388608], P(('gx', 'gy')), may hold values from 0.5 to 2
- move_rows: int32 [2097152], P(('gx', 'gy')), may hold values from 0 to 16383, as said below
- move_slot: int32 [2097152], P(('gx', 'gy')), may hold values from 0 to 8191, as said below
- move_new: int32 [2097152], P(('gx', 'gy')), may hold values from 0 to 16383, as said below
- edge_rows: int32 [4, 524288], P(None, ('gx', 'gy')), may hold values from 0 to 16383
- corner_rows: int32 [4, 32768], P(None, ('gx', 'gy')), may hold values from 0 to 16383
- tile_src: int32 [196608], P(('gx', 'gy')), may hold values from 0 to 161
- bond_bits: int32 [196608, 2048], P(('gx', 'gy')), may hold values from 0 to 255
Outputs:
- speeds_after_update: float32 [2, 8388608], P(None, ('gx', 'gy'))
- moved_offsets_after: float32 [2, 8388608], P(None, ('gx', 'gy'))
The draws below stay inside these ranges and needn't reach their ends.
Inputs may be any that keep to these rules, and one draw needn't show every extreme that they name: `move_rows`: each owner's 4096 entries are distinct rows of its own points. `move_slot`: each owner's entries are distinct; no owner sends more than 256 points to one destination, and every owner sends exactly 256 to some destination. `move_new`: the rows at which an owner receives points are exactly its own move_rows, each once.
All inputs are finite; a program needn't handle non-finite values.
Results may differ from the reference program's by a relative error of at most 0.00002.
Values sent between devices are 32-bit elements; how exact they have to be, the bound alone decides.
No kernel may reach another device: no remote copies, remote signals or barrier semaphores. Data moves between devices by JAX's collectives and lax.ppermute only.
A program may use at most 128 MiB of HBM per device.

```python
import math
import jax
import jax.numpy as jnp
from jax import lax

BLOCK = 128
PER_BLOCK = 3
POINTS_DEV = 16384
MOVERS = 4096
HALO_LEN = 1024
CORNER_LEN = 64
CAPACITY = 256
OWN_BLOCKS = 128
TILES_DEV = 384
EXT_BLOCKS = 162
WORDS = 2048
TOTAL_POINTS = 8388608
HALO_ALL = 524288
CORNER_ALL = 32768
TILES_ALL = 196608
N_GX = 16
N_GY = 32


def rebalance_plan(key):
    key_list = jax.random.split(jax.random.fold_in(key, 11), 3)
    owners = N_GX * N_GY
    leaving = jax.vmap(lambda one_key: jax.random.permutation(one_key, POINTS_DEV))(jax.random.split(key_list[0], owners))
    leaving = leaving.reshape(N_GX, N_GY, POINTS_DEV).astype(jnp.int32)
    arrival = jax.vmap(lambda one_key: jax.random.permutation(one_key, MOVERS))(jax.random.split(key_list[1], owners))
    arrival = arrival.reshape(N_GX, N_GY, MOVERS).astype(jnp.int32)
    offsets = jax.vmap(lambda one_key: jax.random.permutation(one_key, N_GY))(jax.random.split(key_list[2], N_GX))
    offsets = offsets.astype(jnp.int32)
    quarter = N_GY // 4 * CAPACITY
    groups_of = jnp.where(arrival < quarter, arrival // CAPACITY, N_GY // 4 + (arrival - quarter) // (CAPACITY // 2))
    group_start = jnp.where(arrival < quarter, groups_of * CAPACITY, quarter + (groups_of - N_GY // 4) * (CAPACITY // 2))
    offset_table = jnp.broadcast_to(offsets[:, None, :], (N_GX, N_GY, N_GY))
    offset_of = jnp.take_along_axis(offset_table, groups_of, axis=2)
    source_pos = jnp.arange(N_GY, dtype=jnp.int32)[None, :, None]
    destination = (source_pos + offset_of) % N_GY
    slot_ids = destination * CAPACITY + arrival - group_start
    row_ids = jnp.arange(N_GX, dtype=jnp.int32)[:, None, None]
    target_position_index = leaving[row_ids, destination, arrival]
    moving = leaving[:, :, :MOVERS]
    return (moving.reshape(-1).astype(jnp.int32), slot_ids.reshape(-1).astype(jnp.int32), target_position_index.reshape(-1).astype(jnp.int32))


def draw_move_rows(key, part):
    return rebalance_plan(key)[0]


def draw_move_slot(key, part):
    return rebalance_plan(key)[1]


def draw_move_new(key, part):
    return rebalance_plan(key)[2]


def with_ends(result, rng, smallest, high):
    spot = [jax.random.randint(jax.random.fold_in(rng, axis), (), 0, length) for axis, length in enumerate(result.shape)]
    widest = result.shape.index(max(result.shape))
    neighbour = spot[:widest] + [(spot[widest] + 1) % result.shape[widest]] + spot[widest + 1:]
    return result.at[tuple(spot)].set(smallest).at[tuple(neighbour)].set(high)


def shard_levels(stream_key, shape, pieces, low, top_value):
    gain = 1.0
    for position, shards_of in pieces:
        draws = jax.random.uniform(jax.random.fold_in(jax.random.fold_in(stream_key, 6), position), (shards_of,), jnp.float32, low / len(pieces), top_value / len(pieces))
        gain = gain * jnp.repeat(jnp.exp(draws), shape[position] // shards_of).reshape((-1,) + (1,) * (len(shape) - 1 - position))
    return gain


def scatter_about(key, dims, deviation, limit, cuts=(), held_as=jnp.bfloat16):
    drawn = deviation * jax.random.normal(key, dims, jnp.float32)
    if cuts:
        drawn = drawn * shard_levels(key, dims, cuts, -0.22, 0.18)
    return jnp.clip(drawn, -limit, limit).astype(held_as)


def setup_inputs(seed: int = 0) -> dict:
    key_of = jax.random.split(jax.random.key(seed), 13)
    return {
        "positions": jnp.clip(4.0 * jax.random.uniform(key_of[0], (2, TOTAL_POINTS), jnp.float32) ** shard_levels(key_of[0], (2, TOTAL_POINTS), ((1, 512),), -0.2, 0.2), 0.0, 4.0),
        "displacement": scatter_about(key_of[1], (2, TOTAL_POINTS), 1.0, 6.0, ((1, 512),), jnp.float32),
        "velocity": scatter_about(key_of[2], (2, TOTAL_POINTS), 1.0, 6.0, ((1, 512),), jnp.float32),
        "stiffness": jnp.clip(jnp.exp(math.log(4.0) - 2.0794415 * jax.random.uniform(key_of[3], (TOTAL_POINTS,), jnp.float32) ** shard_levels(key_of[3], (TOTAL_POINTS,), ((0, 512),), -0.2, 0.2)), 0.5, 4.0),
        "density": jnp.clip(jnp.exp(math.log(2.0) - 1.3862944 * jax.random.uniform(key_of[4], (TOTAL_POINTS,), jnp.float32) ** shard_levels(key_of[4], (TOTAL_POINTS,), ((0, 512),), -0.2, 0.2)), 0.5, 2.0),
        "move_rows": draw_move_rows(jax.random.fold_in(key_of[12], 71), 0),
        "move_slot": draw_move_slot(jax.random.fold_in(key_of[12], 71), 0),
        "move_new": draw_move_new(jax.random.fold_in(key_of[12], 71), 0),
        "edge_rows": with_ends(jax.random.randint(key_of[8], (4, HALO_ALL), 0, POINTS_DEV), jax.random.fold_in(key_of[8], 1), 0, POINTS_DEV - 1).astype(jnp.int32),
        "corner_rows": with_ends(jax.random.randint(key_of[9], (4, CORNER_ALL), 0, POINTS_DEV), jax.random.fold_in(key_of[9], 1), 0, POINTS_DEV - 1).astype(jnp.int32),
        "tile_src": with_ends(jax.random.randint(key_of[10], (TILES_ALL,), 0, EXT_BLOCKS), jax.random.fold_in(key_of[10], 1), 0, EXT_BLOCKS - 1).astype(jnp.int32),
        "bond_bits": with_ends(jax.random.randint(key_of[11], (TILES_ALL, WORDS), 0, 256), jax.random.fold_in(key_of[11], 1), 0, 255).astype(jnp.int32),
    }


NEAR_FLOOR = 0.5
BOND_COEFFICIENT = 0.005
SHIFT_STEP_SIZE = 0.5
EDGE_DIRS = ((-1, 0), (0, -1), (0, 1), (1, 0))
CORNER_DIRS = ((-1, -1), (-1, 1), (1, -1), (1, 1))

def unpack(bond_words):
    lead = bond_words.shape[:-1]
    rows_words = bond_words.reshape(lead + (BLOCK, BLOCK // 8))
    widened = jnp.repeat(rows_words, 8, axis=-1)
    shifts = jnp.arange(BLOCK, dtype=jnp.int32) % 8
    return jnp.bitwise_and(jnp.right_shift(widened, shifts), 1).astype(jnp.float32)

def tile_forces(target, source, bond_words):
    intact = unpack(bond_words)
    sep_x = source[0][:, None, :] - target[0][:, :, None]
    sep_y = source[1][:, None, :] - target[1][:, :, None]
    rel_x = source[2][:, None, :] - target[2][:, :, None]
    rel_y = source[3][:, None, :] - target[3][:, :, None]
    separation = jnp.sqrt(sep_x * sep_x + sep_y * sep_y)
    inverse = 1.0 / jnp.maximum(separation, NEAR_FLOOR)
    weight = intact * (sep_x * rel_x + sep_y * rel_y) * inverse * inverse * inverse * source[4][:, None, :]
    push_x = lax.optimization_barrier(jnp.sum(weight * sep_x, axis=2)) * target[4]
    push_y = lax.optimization_barrier(jnp.sum(weight * sep_y, axis=2)) * target[4]
    return jnp.stack([push_x, push_y])

def slots_from(owner_grid, lists, directions):
    found = []
    for slot_index in range(4):
        shift_x, shift_y = directions[slot_index]
        outgoing = jnp.take_along_axis(owner_grid, lists[slot_index][None], axis=3)
        padded = jnp.pad(outgoing, ((0, 0), (1, 1), (1, 1), (0, 0)))
        found.append(padded[:, 1 - shift_x:1 - shift_x + N_GX, 1 - shift_y:1 - shift_y + N_GY])
    return found

def reference(positions, displacement, velocity, stiffness, density, move_rows, move_slot, move_new, edge_rows, corner_rows, tile_src, bond_bits):
    ledger_item = jnp.concatenate([positions, displacement, velocity, stiffness[None], density[None]], 0)
    owner_ids = jnp.arange(N_GX * N_GY, dtype=jnp.int32)
    mover_owner = jnp.repeat(owner_ids, MOVERS)
    base_location = mover_owner * POINTS_DEV + move_rows
    dest_owner = mover_owner - mover_owner % N_GY + move_slot // CAPACITY
    target_position_index = dest_owner * POINTS_DEV + move_new
    redistributed_configuration = ledger_item.at[:, target_position_index].set(ledger_item[:, base_location])
    carried_message_content = jnp.concatenate([redistributed_configuration[0:4], jnp.sqrt(redistributed_configuration[6:7])], 0)
    owner_grid = carried_message_content.reshape(5, N_GX, N_GY, POINTS_DEV)
    edge_slots = slots_from(owner_grid, edge_rows.reshape(4, N_GX, N_GY, HALO_LEN), EDGE_DIRS)
    corner_slots = slots_from(owner_grid, corner_rows.reshape(4, N_GX, N_GY, CORNER_LEN), CORNER_DIRS)
    pad_cols = EXT_BLOCKS * BLOCK - POINTS_DEV - 4 * HALO_LEN - 4 * CORNER_LEN
    filler = jnp.zeros((5, N_GX, N_GY, pad_cols), jnp.float32)
    extended = jnp.concatenate([owner_grid] + edge_slots + corner_slots + [filler], 3)
    extended = extended.reshape(5, N_GX * N_GY, EXT_BLOCKS, BLOCK)
    extended = jnp.moveaxis(extended, 1, 0)

    def one_owner(operands):
        owner_ext, source_ids, bond_words = operands
        target = jnp.repeat(owner_ext[:, :OWN_BLOCKS], PER_BLOCK, axis=1)
        pushes = tile_forces(target, owner_ext[:, source_ids], bond_words)
        return pushes.reshape(2, OWN_BLOCKS, PER_BLOCK, BLOCK).sum(2).reshape(2, POINTS_DEV)
    summed_pull = lax.map(one_owner, (extended, tile_src.reshape(-1, TILES_DEV), bond_bits.reshape(-1, TILES_DEV, WORDS)))
    summed_pull = jnp.moveaxis(summed_pull, 0, 1).reshape(2, TOTAL_POINTS)
    speeds_after_update = redistributed_configuration[4:6] + BOND_COEFFICIENT * summed_pull / redistributed_configuration[7]
    moved_offsets_after = redistributed_configuration[2:4] + SHIFT_STEP_SIZE * speeds_after_update
    return (speeds_after_update, moved_offsets_after)
```

```python
import functools

import jax
import jax.numpy as jnp
from jax import lax
from jax.experimental import pallas as pl
from jax.experimental.pallas import tpu as pltpu
from jax.sharding import PartitionSpec as P

F32 = jnp.float32
BF16 = jnp.bfloat16
I32 = jnp.int32

LANES = 128
PER_BLOCK = 3
NEAR_FLOOR = 0.5
BOND_COEFFICIENT = 0.005
SHIFT_STEP_SIZE = 0.5

PARTS = 3
SEND_ROWS = 24
SLOTS = 256
UNROLL = 4
VMEM_LIMIT = 56 * 1024 * 1024


def passed_along(block, axis, distance):
    devices = range(lax.axis_size(axis))
    route = [(i - distance, i) for i in devices if i - distance in devices]
    return lax.ppermute(block, axis, route)


def split(x):
    parts = []
    for _ in range(PARTS):
        part = x.astype(BF16)
        parts.append(part)
        x = x - part.astype(F32)
    return parts


def iota(shape, dim):
    return lax.broadcasted_iota(I32, shape, dim)


def ones_where(mask):
    return jnp.where(mask, 1.0, 0.0).astype(BF16)


def lookup_table(table, comp, x):
    for s, part in enumerate(split(x.T)):
        table[comp * LANES : (comp + 1) * LANES, s * LANES : (s + 1) * LANES] = part


def looked_up(table, comps, index):
    width = index.shape[1]
    high = ones_where(iota((LANES, width), 0) == (index >> 7))
    low = iota((LANES, width), 0) == (index & 127)
    found = jnp.dot(table[...], jnp.concatenate([high] * PARTS, 0), preferred_element_type=F32)
    return [
        jnp.sum(jnp.where(low, found[c * LANES : (c + 1) * LANES], 0.0), axis=0, keepdims=True)
        for c in range(comps)
    ]


def two_rows(ref, first):
    return jnp.concatenate([ref[pl.ds(first, 1), :], ref[pl.ds(first + 1, 1), :]], 1)


NT = (((1,), (1,)), ((), ()))


def send_kernel(pos, dis, vel, sti, den, rows, slots, news, out, table, spread, total):
    for c, ref in enumerate((pos, dis, vel)):
        for d in range(2):
            lookup_table(table, 2 * c + d, ref[pl.ds(d, LANES, stride=2), :])
    lookup_table(table, 6, sti[...])
    lookup_table(table, 7, den[...])
    total[...] = jnp.zeros_like(total)
    owners = out.shape[0] // SEND_ROWS

    @pl.loop(0, rows.shape[0] // 2)
    def _(k):
        index = two_rows(rows, 2 * k)
        slot = two_rows(slots, 2 * k)
        new = two_rows(news, 2 * k)
        values = looked_up(table, 8, index)
        values.append((new + 1).astype(F32))
        here = iota((owners, SLOTS), 0) == (slot >> 8)
        for c, value in enumerate(values):
            for s, part in enumerate(split(value)):
                at = (s * 9 + c) * owners
                spread[at : at + owners, :] = jnp.where(here, part.astype(F32), 0.0).astype(BF16)
        place = ones_where(iota((SLOTS, SLOTS), 0) == (slot & 255))
        total[...] += lax.dot_general(spread[...], place, NT, preferred_element_type=F32)

    out[...] = jnp.zeros_like(out)
    for c in range(9):
        value = total[c * owners : (c + 1) * owners, :]
        for s in range(1, PARTS):
            value = value + total[(s * 9 + c) * owners : (s * 9 + c + 1) * owners, :]
        out[pl.ds(2 * c, owners, stride=SEND_ROWS), :] = value[:, :LANES]
        out[pl.ds(2 * c + 1, owners, stride=SEND_ROWS), :] = value[:, LANES:]


def receive_kernel(
    got, pos, dis, vel, sti, den, edge_rows, corner_rows, record, *rest
):
    bundles, (table, spread, place, total) = rest[:4], rest[4:]
    owners = got.shape[0] // SEND_ROWS
    batch = place.shape[1] // SLOTS
    total[...] = jnp.zeros_like(total)

    @pl.loop(0, owners // batch)
    def _(k):
        for i in range(batch):
            first = (k * batch + i) * SEND_ROWS
            at_lanes = slice(i * SLOTS, (i + 1) * SLOTS)
            row = two_rows(got, first + 16).astype(I32) - 1
            here = iota((64, SLOTS), 0) == (row >> 8)
            for c in range(8):
                for s, part in enumerate(split(two_rows(got, first + 2 * c))):
                    at = (s * 8 + c) * 64
                    spread[at : at + 64, at_lanes] = jnp.where(
                        here, part.astype(F32), 0.0
                    ).astype(BF16)
            place[:, at_lanes] = ones_where(iota((256, SLOTS), 0) == (row & 255))
        total[...] += lax.dot_general(spread[...], place[...], NT, preferred_element_type=F32)

    def arrived(c):
        value = total[c * 64 : (c + 1) * 64, :]
        for s in range(1, PARTS):
            value = value + total[(s * 8 + c) * 64 : (s * 8 + c + 1) * 64, :]
        return value

    moved = arrived(6) > 0.25
    for c in range(8):
        value = arrived(c)
        for half in range(2):
            if c < 6:
                ref = (pos, dis, vel)[c // 2]
                kept = ref[pl.ds(2 * half + c % 2, 64, stride=4), :]
            else:
                kept = (sti, den)[c - 6][pl.ds(half, 64, stride=2), :]
            lanes = slice(half * LANES, (half + 1) * LANES)
            chosen = jnp.where(moved[:, lanes], value[:, lanes], kept)
            if c == 6:
                chosen = jnp.sqrt(chosen)
            record[pl.ds(c * LANES + half, 64, stride=2), :] = chosen
    for c, source in enumerate((0, 1, 2, 3, 6)):
        lookup_table(table, c, record[source * LANES : (source + 1) * LANES, :])
    for edge, bundle in zip((0, 3, 1, 2), bundles):

        @pl.loop(0, edge_rows.shape[1] // 256)
        def _(q):
            index = edge_rows[edge : edge + 1, pl.ds(pl.multiple_of(q * 256, 256), 256)]
            for c, value in enumerate(looked_up(table, 5, index)):
                bundle[pl.ds(c * 8 + 2 * q, 1), :] = value[:, :LANES]
                bundle[pl.ds(c * 8 + 2 * q + 1, 1), :] = value[:, LANES:]

    corners = corner_rows[...]
    index = jnp.concatenate([corners[i : i + 1, :] for i in range(4)], 1)
    for b in range(2):
        bundles[b][40:48, :] = jnp.zeros((8, LANES), F32)
    for c, value in enumerate(looked_up(table, 5, index)):
        bundles[0][40 + c : 41 + c, :] = value[:, :LANES]
        bundles[1][40 + c : 41 + c, :] = value[:, LANES:]


def list_kernel(source, near_tile, near_source, far_tile, far_source, counts):
    tiles = source.shape[0]

    def step(t, carry):
        near, far = carry
        src = source[t]
        near_tile[near] = t
        near_source[near] = src
        far_tile[far] = t
        far_source[far] = src
        is_near = (src < LANES).astype(I32)
        return near + is_near, far + 1 - is_near

    near, far = lax.fori_loop(0, tiles, step, (jnp.int32(0), jnp.int32(0)))
    for i in range(UNROLL):
        near_tile[near + i] = tiles
        near_source[near + i] = 0
        far_tile[far + i] = tiles
        far_source[far + i] = LANES
    counts[0] = (near + UNROLL - 1) // UNROLL
    counts[1] = (far + UNROLL - 1) // UNROLL


def expand_targets(record, targets):
    parts = [
        jnp.concatenate(split(record[c * LANES : (c + 1) * LANES, :]), 1) for c in range(4)
    ]
    values = jnp.concatenate(parts, 0)
    for r in range(0, 16, 2):
        shape = (LANES, 2 * LANES)
        lane = iota(shape, 1)
        chosen = ones_where(iota(shape, 0) == 8 * r + lane // 16)
        spread = jnp.dot(
            values, jnp.concatenate([chosen] * PARTS, 0), preferred_element_type=F32
        )
        for c in range(4):
            for half in range(2):
                targets[pl.ds(c * 16 + r + half, LANES, stride=64), :] = spread[
                    c * LANES : (c + 1) * LANES, half * LANES : (half + 1) * LANES
                ]


def expand_sources(arrays, sources):
    count = arrays[0].shape[0]
    values = jnp.concatenate([jnp.concatenate(split(a), 1) for a in arrays], 0)
    for b in range(0, 8, 2):
        shape = (LANES, 2 * LANES)
        lane = iota(shape, 1)
        chosen = ones_where(iota(shape, 0) == 8 * (lane % 16) + b + lane // LANES)
        spread = jnp.dot(
            values, jnp.concatenate([chosen] * PARTS, 0), preferred_element_type=F32
        )
        for c in range(5):
            for half in range(2):
                value = spread[c * count : (c + 1) * count, half * LANES : (half + 1) * LANES]
                if c == 4:
                    value = value * (2.0 ** -(b + half))
                sources[pl.ds(c * 8 + b + half, count, stride=40), :] = value


def tile_loop(steps, tile_ids, tile_sources, first_block, words, targets, sources, pushed):
    tiles = words.shape[0] // 16

    def one_tile(position):
        tile = tile_ids[position]
        base = (tile_sources[position] - first_block) * 40
        known = jnp.minimum(tile, tiles - 1)
        word = words[pl.ds((known >> 3) * LANES + (known & 7), 16, stride=8), :]
        block = pl.multiple_of(((known * 43691) >> 17) * 64, 64)
        tx, ty, tu, tv = (targets[pl.ds(block + 16 * c, 16), :] for c in range(4))
        push_x = push_y = None
        for b in range(8):
            sx, sy, su, sv, root = (
                sources[pl.ds(base + 8 * c + b, 1), :] for c in range(5)
            )
            sep_x, sep_y = sx - tx, sy - ty
            rel_x, rel_y = su - tu, sv - tv
            square = sep_x * sep_x + sep_y * sep_y
            inverse = lax.rsqrt(jnp.maximum(square, NEAR_FLOOR * NEAR_FLOOR))
            intact = (word & (1 << b)).astype(F32)
            weight = (
                (sep_x * rel_x + sep_y * rel_y)
                * (inverse * inverse)
                * (inverse * root)
                * intact
            )
            more_x, more_y = weight * sep_x, weight * sep_y
            push_x = more_x if b == 0 else push_x + more_x
            push_y = more_y if b == 0 else push_y + more_y
        return tile, push_x, push_y

    @pl.loop(0, steps)
    def _(step):
        for tile, push_x, push_y in [one_tile(step * UNROLL + i) for i in range(UNROLL)]:
            at = pl.multiple_of(tile * 32, 32)
            pushed[pl.ds(at, 16), :] = push_x
            pushed[pl.ds(at + 16, 16), :] = push_y


def gathered_force(pushed, comp, blocks):
    stride = 32 * PER_BLOCK
    total = None
    for r in range(16):
        value = None
        for k in range(PER_BLOCK):
            part = pushed[pl.ds(32 * k + 16 * comp + r, blocks, stride=stride), :]
            value = part if value is None else value + part
        shape = (LANES, LANES)
        chosen = ones_where(iota(shape, 1) == 8 * r + iota(shape, 0) // 16)
        more = jnp.dot(
            jnp.concatenate(split(value), 1),
            jnp.concatenate([chosen] * PARTS, 0),
            preferred_element_type=F32,
        )
        total = more if total is None else total + more
    return total


def near_kernel(tile_ids, tile_sources, counts, record, words, force, targets, sources, pushed):
    pushed[...] = jnp.zeros_like(pushed)
    expand_targets(record, targets)
    expand_sources(
        [record[c * LANES : (c + 1) * LANES, :] for c in (0, 1, 2, 3, 6)], sources
    )
    tile_loop(counts[0], tile_ids, tile_sources, 0, words, targets, sources, pushed)
    for d in range(2):
        force[d * LANES : (d + 1) * LANES, :] = gathered_force(pushed, d, LANES)


def far_kernel(
    tile_ids, tile_sources, counts, record, words, force, x_low, x_high, y_low, y_high,
    speeds, offsets, targets, sources, pushed
):
    pushed[...] = jnp.zeros_like(pushed)
    expand_targets(record, targets)
    halo = []
    left = iota((1, LANES), 1) < 64
    for c in range(5):
        edges = [ref[8 * c : 8 * c + 8, :] for ref in (x_low, y_low, y_high, x_high)]
        corners = [
            jnp.where(left, y_low[r + c : r + c + 1, :], y_high[r + c : r + c + 1, :])
            for r in (40, 48)
        ]
        halo.append(jnp.concatenate(edges + corners + [jnp.zeros((6, LANES), F32)], 0))
    expand_sources(halo, sources)
    tile_loop(counts[1], tile_ids, tile_sources, LANES, words, targets, sources, pushed)
    root = record[6 * LANES : 7 * LANES, :]
    density = record[7 * LANES : 8 * LANES, :]
    for d in range(2):
        total = force[d * LANES : (d + 1) * LANES, :] + gathered_force(pushed, d, LANES)
        speed = record[(4 + d) * LANES : (5 + d) * LANES, :] + (
            BOND_COEFFICIENT * (total * root) / density
        )
        speeds[pl.ds(d, LANES, stride=2), :] = speed
        offsets[pl.ds(d, LANES, stride=2), :] = (
            record[(2 + d) * LANES : (3 + d) * LANES, :] + SHIFT_STEP_SIZE * speed
        )


VM = pl.BlockSpec(memory_space=pltpu.VMEM)
SM = pl.BlockSpec(memory_space=pltpu.SMEM)


def call(kernel, in_specs, outs, scratch, name, flops=0, moved=0):
    return pl.pallas_call(
        kernel,
        name=name,
        in_specs=in_specs,
        out_specs=[spec for spec, _, _ in outs],
        out_shape=[jax.ShapeDtypeStruct(shape, dtype) for _, shape, dtype in outs],
        scratch_shapes=[pltpu.VMEM(shape, dtype) for shape, dtype in scratch],
        cost_estimate=pl.CostEstimate(flops=flops, bytes_accessed=moved, transcendentals=0),
        compiler_params=pltpu.CompilerParams(vmem_limit_bytes=VMEM_LIMIT),
    )


def pair_rows(x):
    return x.reshape(2, LANES, LANES).transpose(1, 0, 2).reshape(2 * LANES, LANES)


def unpair_rows(x):
    return x.reshape(LANES, 2, LANES).transpose(1, 0, 2).reshape(2, LANES * LANES)


def body(
    positions,
    displacement,
    velocity,
    stiffness,
    density,
    move_rows,
    move_slot,
    move_new,
    edge_rows,
    corner_rows,
    tile_src,
    bond_bits,
):
    owners = lax.axis_size("gy")
    tiles = tile_src.shape[0]
    state = (
        pair_rows(positions),
        pair_rows(displacement),
        pair_rows(velocity),
        stiffness.reshape(LANES, LANES),
        density.reshape(LANES, LANES),
    )
    moves = tuple(m.reshape(-1, LANES) for m in (move_rows, move_slot, move_new))
    words = (
        bond_bits.reshape(tiles // 8, 8, 16, LANES).transpose(0, 2, 1, 3).reshape(-1, LANES)
    )

    (outgoing,) = call(
        send_kernel,
        [VM] * 8,
        [(VM, (owners * SEND_ROWS, LANES), F32)],
        [
            ((8 * LANES, PARTS * LANES), BF16),
            ((PARTS * 9 * owners, SLOTS), BF16),
            ((PARTS * 9 * owners, SLOTS), F32),
        ],
        "send",
    )(*state, *moves)
    got = lax.all_to_all(
        outgoing.reshape(owners, SEND_ROWS, LANES), "gy", split_axis=0, concat_axis=0, tiled=True
    ).reshape(owners * SEND_ROWS, LANES)

    listed = tiles + UNROLL
    near_tile, near_source, far_tile, far_source, counts = call(
        list_kernel,
        [SM],
        [(SM, (listed,), I32)] * 4 + [(SM, (2,), I32)],
        [],
        "lists",
    )(tile_src)

    batch = 4
    record, x_low, x_high, y_low, y_high = call(
        receive_kernel,
        [VM] * 8,
        [(VM, (8 * LANES, LANES), F32)]
        + [(VM, (48, LANES), F32)] * 2
        + [(VM, (40, LANES), F32)] * 2,
        [
            ((5 * LANES, PARTS * LANES), BF16),
            ((PARTS * 8 * 64, batch * SLOTS), BF16),
            ((256, batch * SLOTS), BF16),
            ((PARTS * 8 * 64, 256), F32),
        ],
        "receive",
    )(got, *state, edge_rows, corner_rows)

    x_low = passed_along(x_low, "gx", -1)
    x_high = passed_along(x_high, "gx", 1)
    corners = [x_low[40:], x_high[40:]]
    y_low = passed_along(jnp.concatenate([y_low] + corners, 0), "gy", -1)
    y_high = passed_along(jnp.concatenate([y_high] + corners, 0), "gy", 1)

    (force,) = call(
        near_kernel,
        [SM] * 3 + [VM] * 2,
        [(VM, (2 * LANES, LANES), F32)],
        [
            ((64 * LANES, LANES), F32),
            ((40 * LANES, LANES), F32),
            ((32 * (tiles + 1), LANES), F32),
        ],
        "near",
        flops=10**9,
        moved=10**8,
    )(near_tile, near_source, counts, record, words)
    speeds, offsets = call(
        far_kernel,
        [SM] * 3 + [VM] * 7,
        [(VM, (2 * LANES, LANES), F32)] * 2,
        [
            ((64 * LANES, LANES), F32),
            ((40 * 40, LANES), F32),
            ((32 * (tiles + 1), LANES), F32),
        ],
        "far",
    )(far_tile, far_source, counts, record, words, force, x_low, x_high, y_low, y_high)
    return unpair_rows(speeds), unpair_rows(offsets)


def solution(mesh):
    placed = (
        P(None, ("gx", "gy")),
        P(None, ("gx", "gy")),
        P(None, ("gx", "gy")),
        P(("gx", "gy")),
        P(("gx", "gy")),
        P(("gx", "gy")),
        P(("gx", "gy")),
        P(("gx", "gy")),
        P(None, ("gx", "gy")),
        P(None, ("gx", "gy")),
        P(("gx", "gy")),
        P(("gx", "gy"), None),
    )
    return jax.shard_map(
        body,
        mesh=mesh,
        in_specs=placed,
        out_specs=(P(None, ("gx", "gy")), P(None, ("gx", "gy"))),
        check_vma=False,
    )
```

```python
import functools

import jax
import jax.numpy as jnp
from jax import lax
from jax.experimental import pallas as pl
from jax.experimental.pallas import tpu as pltpu
from jax.sharding import PartitionSpec as P

F32 = jnp.float32
BF16 = jnp.bfloat16
I32 = jnp.int32

LANES = 128
PER_BLOCK = 3
NEAR_FLOOR = 0.5
BOND_COEFFICIENT = 0.005
SHIFT_STEP_SIZE = 0.5

PARTS = 3
SEND_ROWS = 24
SLOTS = 256
UNROLL = 4
TARGET_ROWS = 72
VMEM_LIMIT = 56 * 1024 * 1024


def passed_along(block, axis, distance):
    devices = range(lax.axis_size(axis))
    route = [(i - distance, i) for i in devices if i - distance in devices]
    return lax.ppermute(block, axis, route)


def split(x):
    parts = []
    for _ in range(PARTS):
        part = x.astype(BF16)
        parts.append(part)
        x = x - part.astype(F32)
    return parts


def iota(shape, dim):
    return lax.broadcasted_iota(I32, shape, dim)


def ones_where(mask):
    return jnp.where(mask, 1.0, 0.0).astype(BF16)


def lookup_table(table, comp, x):
    turned = x.T
    turned = jnp.concatenate([turned[:64], turned[64:]], 1)
    for s, part in enumerate(split(turned)):
        table[comp * 64 : (comp + 1) * 64, s * 256 : (s + 1) * 256] = part


def looked_up(table, comps, index):
    width = index.shape[1]
    high = ones_where(iota((256, width), 0) == ((index >> 7) + ((index & 64) << 1)))
    low = iota((64, width), 0) == (index & 63)
    found = jnp.dot(table[...], jnp.concatenate([high] * PARTS, 0), preferred_element_type=F32)
    return [
        jnp.sum(jnp.where(low, found[c * 64 : (c + 1) * 64], 0.0), axis=0, keepdims=True)
        for c in range(comps)
    ]


def two_rows(ref, first):
    return jnp.concatenate([ref[pl.ds(first, 1), :], ref[pl.ds(first + 1, 1), :]], 1)


NT = (((1,), (1,)), ((), ()))


def send_kernel(
    source, pos, dis, vel, sti, den, rows, slots, news,
    out, near_tile, near_source, far_tile, far_source, counts,
    table, spread, place, total
):
    for c, ref in enumerate((pos, dis, vel)):
        for d in range(2):
            lookup_table(table, 2 * c + d, ref[pl.ds(d, LANES, stride=2), :])
    lookup_table(table, 6, sti[...])
    lookup_table(table, 7, den[...])
    total[...] = jnp.zeros_like(total)
    owners = out.shape[0] // SEND_ROWS
    tiles = source.shape[0]
    batch = place.shape[1] // SLOTS
    steps = rows.shape[0] // 2 // batch

    def step(k, carry):
        near, far = carry
        for i in range(tiles // steps):
            tile = k * (tiles // steps) + i
            src = source[tile]
            near_tile[near] = tile
            near_source[near] = src
            far_tile[far] = tile
            far_source[far] = src
            is_near = (src < LANES).astype(I32)
            near, far = near + is_near, far + 1 - is_near
        for i in range(batch):
            first = 2 * (k * batch + i)
            at_lanes = slice(i * SLOTS, (i + 1) * SLOTS)
            index = two_rows(rows, first)
            slot = two_rows(slots, first)
            new = two_rows(news, first)
            values = looked_up(table, 8, index)
            values.append((new + 1).astype(F32))
            here = iota((owners, SLOTS), 0) == (slot >> 8)
            for c, value in enumerate(values):
                for s, part in enumerate(split(value)):
                    at = (s * 9 + c) * owners
                    spread[at : at + owners, at_lanes] = jnp.where(
                        here, part.astype(F32), 0.0
                    ).astype(BF16)
            place[:, at_lanes] = ones_where(iota((SLOTS, SLOTS), 0) == (slot & 255))
        total[...] += lax.dot_general(spread[...], place[...], NT, preferred_element_type=F32)
        return near, far

    near, far = lax.fori_loop(0, steps, step, (jnp.int32(0), jnp.int32(0)))
    for i in range(UNROLL):
        near_tile[near + i] = tiles
        near_source[near + i] = 0
        far_tile[far + i] = tiles
        far_source[far + i] = LANES
    counts[0] = (near + UNROLL - 1) // UNROLL
    counts[1] = (far + UNROLL - 1) // UNROLL

    out[...] = jnp.zeros_like(out)
    for c in range(9):
        value = total[c * owners : (c + 1) * owners, :]
        for s in range(1, PARTS):
            value = value + total[(s * 9 + c) * owners : (s * 9 + c + 1) * owners, :]
        out[pl.ds(2 * c, owners, stride=SEND_ROWS), :] = value[:, :LANES]
        out[pl.ds(2 * c + 1, owners, stride=SEND_ROWS), :] = value[:, LANES:]


def receive_kernel(
    got, pos, dis, vel, sti, den, edge_rows, corner_rows, record, *rest
):
    bundles, (table, spread, place, total) = rest[:4], rest[4:]
    owners = got.shape[0] // SEND_ROWS
    batch = place.shape[1] // SLOTS
    total[...] = jnp.zeros_like(total)

    @pl.loop(0, owners // batch)
    def _(k):
        for i in range(batch):
            first = (k * batch + i) * SEND_ROWS
            at_lanes = slice(i * SLOTS, (i + 1) * SLOTS)
            row = two_rows(got, first + 16).astype(I32) - 1
            here = iota((64, SLOTS), 0) == (row >> 8)
            for c in range(8):
                for s, part in enumerate(split(two_rows(got, first + 2 * c))):
                    at = (s * 8 + c) * 64
                    spread[at : at + 64, at_lanes] = jnp.where(
                        here, part.astype(F32), 0.0
                    ).astype(BF16)
            place[:, at_lanes] = ones_where(iota((256, SLOTS), 0) == (row & 255))
        total[...] += lax.dot_general(spread[...], place[...], NT, preferred_element_type=F32)

    def arrived(c):
        value = total[c * 64 : (c + 1) * 64, :]
        for s in range(1, PARTS):
            value = value + total[(s * 8 + c) * 64 : (s * 8 + c + 1) * 64, :]
        return value

    moved = arrived(6) > 0.25
    for c in range(8):
        value = arrived(c)
        for half in range(2):
            if c < 6:
                ref = (pos, dis, vel)[c // 2]
                kept = ref[pl.ds(2 * half + c % 2, 64, stride=4), :]
            else:
                kept = (sti, den)[c - 6][pl.ds(half, 64, stride=2), :]
            lanes = slice(half * LANES, (half + 1) * LANES)
            chosen = jnp.where(moved[:, lanes], value[:, lanes], kept)
            if c == 6:
                chosen = jnp.sqrt(chosen)
            record[pl.ds(c * LANES + half, 64, stride=2), :] = chosen
    for c, source in enumerate((0, 1, 2, 3, 6)):
        lookup_table(table, c, record[source * LANES : (source + 1) * LANES, :])
    @pl.loop(0, edge_rows.shape[1] // 256)
    def _(q):
        for edge, bundle in zip((0, 3, 1, 2), bundles):
            index = edge_rows[edge : edge + 1, pl.ds(pl.multiple_of(q * 256, 256), 256)]
            for c, value in enumerate(looked_up(table, 5, index)):
                bundle[pl.ds(c * 8 + 2 * q, 1), :] = value[:, :LANES]
                bundle[pl.ds(c * 8 + 2 * q + 1, 1), :] = value[:, LANES:]

    corners = corner_rows[...]
    index = jnp.concatenate([corners[i : i + 1, :] for i in range(4)], 1)
    for b in range(2):
        bundles[b][40:48, :] = jnp.zeros((8, LANES), F32)
    for c, value in enumerate(looked_up(table, 5, index)):
        bundles[0][40 + c : 41 + c, :] = value[:, :LANES]
        bundles[1][40 + c : 41 + c, :] = value[:, LANES:]


def expand_targets(record, targets):
    parts = [
        jnp.concatenate(split(record[c * LANES : (c + 1) * LANES, :]), 1) for c in range(4)
    ]
    values = jnp.concatenate(parts, 0)
    for r in range(0, 16, 2):
        shape = (LANES, 2 * LANES)
        lane = iota(shape, 1)
        chosen = ones_where(iota(shape, 0) == 8 * r + lane // 16)
        spread = jnp.dot(
            values, jnp.concatenate([chosen] * PARTS, 0), preferred_element_type=F32
        )
        for c in range(4):
            for half in range(2):
                targets[pl.ds(c * 16 + r + half, LANES, stride=TARGET_ROWS), :] = spread[
                    c * LANES : (c + 1) * LANES, half * LANES : (half + 1) * LANES
                ]


def expand_sources(arrays, sources):
    count = arrays[0].shape[0]
    values = jnp.concatenate([jnp.concatenate(split(a), 1) for a in arrays], 0)
    for b in range(0, 8, 2):
        shape = (LANES, 2 * LANES)
        lane = iota(shape, 1)
        chosen = ones_where(iota(shape, 0) == 8 * (lane % 16) + b + lane // LANES)
        spread = jnp.dot(
            values, jnp.concatenate([chosen] * PARTS, 0), preferred_element_type=F32
        )
        for c in range(5):
            for half in range(2):
                value = spread[c * count : (c + 1) * count, half * LANES : (half + 1) * LANES]
                if c == 4:
                    value = value * (2.0 ** -(b + half))
                sources[pl.ds(c * 8 + b + half, count, stride=40), :] = value


def tile_loop(steps, tile_ids, tile_sources, first_block, words, targets, sources, pushed):
    tiles = words.shape[0] // 16

    def one_tile(position):
        tile = tile_ids[position]
        base = (tile_sources[position] - first_block) * 40
        known = jnp.minimum(tile, tiles - 1)
        word = words[pl.ds((known >> 3) * LANES + (known & 7), 16, stride=8), :]
        block = pl.multiple_of(((known * 43691) >> 17) * TARGET_ROWS, 8)
        tx, ty, tu, tv = (targets[pl.ds(block + 16 * c, 16), :] for c in range(4))
        push_x = push_y = None
        for b in range(8):
            sx, sy, su, sv, root = (
                sources[pl.ds(base + 8 * c + b, 1), :] for c in range(5)
            )
            sep_x, sep_y = sx - tx, sy - ty
            rel_x, rel_y = su - tu, sv - tv
            square = sep_x * sep_x + sep_y * sep_y
            inverse = lax.rsqrt(jnp.maximum(square, NEAR_FLOOR * NEAR_FLOOR))
            intact = (word & (1 << b)).astype(F32)
            weight = (
                (sep_x * rel_x + sep_y * rel_y)
                * (inverse * inverse)
                * (inverse * root)
                * intact
            )
            more_x, more_y = weight * sep_x, weight * sep_y
            push_x = more_x if b == 0 else push_x + more_x
            push_y = more_y if b == 0 else push_y + more_y
        return tile, push_x, push_y

    @pl.loop(0, steps)
    def _(step):
        for tile, push_x, push_y in [one_tile(step * UNROLL + i) for i in range(UNROLL)]:
            at = pl.multiple_of(tile * 32, 32)
            pushed[pl.ds(at, 16), :] = push_x
            pushed[pl.ds(at + 16, 16), :] = push_y


def gather_force(pushed, force):
    many = 64
    shape = (LANES, LANES)
    chosen = ones_where(iota(shape, 0) // 16 == iota(shape, 1) % 8)
    chosen = jnp.concatenate([chosen] * PARTS, 0)
    own = iota((16, LANES), 1) // 8 == iota((16, LANES), 0)

    @pl.loop(0, force.shape[0] // 2 // many)
    def _(group):
        values = []
        for i in range(many):
            at = pl.multiple_of((group * many + i) * 32 * PER_BLOCK, 32)
            value = pushed[pl.ds(at, 32), :]
            for k in range(1, PER_BLOCK):
                value = value + pushed[pl.ds(at + 32 * k, 32), :]
            values.append(jnp.concatenate(split(value), 1))
        sums = jnp.dot(jnp.concatenate(values, 0), chosen, preferred_element_type=F32)
        sums = jnp.where(own[None], sums.reshape(2 * many, 16, LANES), 0.0)
        force[pl.ds(pl.multiple_of(group * 2 * many, 2 * many), 2 * many), :] = jnp.sum(sums, axis=1)


def near_kernel(
    tile_ids, tile_sources, counts, record, bonds, force, words, sem, targets, sources, pushed
):
    copy = pltpu.make_async_copy(bonds, words, sem)
    copy.start()
    pushed[...] = jnp.zeros_like(pushed)
    expand_targets(record, targets)
    expand_sources(
        [record[c * LANES : (c + 1) * LANES, :] for c in (0, 1, 2, 3, 6)], sources
    )
    copy.wait()
    tile_loop(counts[0], tile_ids, tile_sources, 0, words, targets, sources, pushed)
    gather_force(pushed, force)


def far_kernel(
    tile_ids, tile_sources, counts, record, bonds, force, x_low, x_high, y_low, y_high,
    speeds, offsets, words, sem, more, targets, sources, pushed
):
    copy = pltpu.make_async_copy(bonds, words, sem)
    copy.start()
    pushed[...] = jnp.zeros_like(pushed)
    expand_targets(record, targets)
    halo = []
    left = iota((1, LANES), 1) < 64
    for c in range(5):
        edges = [ref[8 * c : 8 * c + 8, :] for ref in (x_low, y_low, y_high, x_high)]
        corners = [
            jnp.where(left, y_low[r + c : r + c + 1, :], y_high[r + c : r + c + 1, :])
            for r in (40, 48)
        ]
        halo.append(jnp.concatenate(edges + corners + [jnp.zeros((6, LANES), F32)], 0))
    expand_sources(halo, sources)
    copy.wait()
    tile_loop(counts[1], tile_ids, tile_sources, LANES, words, targets, sources, pushed)
    gather_force(pushed, more)
    root = record[6 * LANES : 7 * LANES, :]
    density = record[7 * LANES : 8 * LANES, :]
    for d in range(2):
        at = pl.ds(d, LANES, stride=2)
        total = force[at, :] + more[at, :]
        speed = record[(4 + d) * LANES : (5 + d) * LANES, :] + (
            BOND_COEFFICIENT * (total * root) / density
        )
        speeds[at, :] = speed
        offsets[at, :] = (
            record[(2 + d) * LANES : (3 + d) * LANES, :] + SHIFT_STEP_SIZE * speed
        )


VM = pl.BlockSpec(memory_space=pltpu.VMEM)
SM = pl.BlockSpec(memory_space=pltpu.SMEM)
HBM = pl.BlockSpec(memory_space=pl.ANY)


def call(kernel, in_specs, outs, scratch, name, flops=0, moved=0):
    return pl.pallas_call(
        kernel,
        name=name,
        in_specs=in_specs,
        out_specs=[spec for spec, _, _ in outs],
        out_shape=[jax.ShapeDtypeStruct(shape, dtype) for _, shape, dtype in outs],
        scratch_shapes=[
            pltpu.SemaphoreType.DMA if not entry else pltpu.VMEM(*entry) for entry in scratch
        ],
        cost_estimate=pl.CostEstimate(flops=flops, bytes_accessed=moved, transcendentals=0),
        compiler_params=pltpu.CompilerParams(vmem_limit_bytes=VMEM_LIMIT),
    )


def pair_rows(x):
    return x.reshape(2, LANES, LANES).transpose(1, 0, 2).reshape(2 * LANES, LANES)


def unpair_rows(x):
    return x.reshape(LANES, 2, LANES).transpose(1, 0, 2).reshape(2, LANES * LANES)


def body(
    positions,
    displacement,
    velocity,
    stiffness,
    density,
    move_rows,
    move_slot,
    move_new,
    edge_rows,
    corner_rows,
    tile_src,
    bond_bits,
):
    owners = lax.axis_size("gy")
    tiles = tile_src.shape[0]
    state = (
        pair_rows(positions),
        pair_rows(displacement),
        pair_rows(velocity),
        stiffness.reshape(LANES, LANES),
        density.reshape(LANES, LANES),
    )
    moves = tuple(m.reshape(-1, LANES) for m in (move_rows, move_slot, move_new))
    words = (
        bond_bits.reshape(tiles // 8, 8, 16, LANES).transpose(0, 2, 1, 3).reshape(-1, LANES)
    )

    batch = 4
    listed = tiles + UNROLL
    outgoing, near_tile, near_source, far_tile, far_source, counts = call(
        send_kernel,
        [SM] + [VM] * 8,
        [(VM, (owners * SEND_ROWS, LANES), F32)]
        + [(SM, (listed,), I32)] * 4
        + [(SM, (2,), I32)],
        [
            ((8 * 64, PARTS * 256), BF16),
            ((PARTS * 9 * owners, batch * SLOTS), BF16),
            ((SLOTS, batch * SLOTS), BF16),
            ((PARTS * 9 * owners, SLOTS), F32),
        ],
        "send",
    )(tile_src, *state, *moves)
    got = lax.all_to_all(
        outgoing.reshape(owners, SEND_ROWS, LANES), "gy", split_axis=0, concat_axis=0, tiled=True
    ).reshape(owners * SEND_ROWS, LANES)

    record, x_low, x_high, y_low, y_high = call(
        receive_kernel,
        [VM] * 8,
        [(VM, (8 * LANES, LANES), F32)]
        + [(VM, (48, LANES), F32)] * 2
        + [(VM, (40, LANES), F32)] * 2,
        [
            ((5 * 64, PARTS * 256), BF16),
            ((PARTS * 8 * 64, batch * SLOTS), BF16),
            ((256, batch * SLOTS), BF16),
            ((PARTS * 8 * 64, 256), F32),
        ],
        "receive",
    )(got, *state, edge_rows, corner_rows)

    x_low = passed_along(x_low, "gx", -1)
    x_high = passed_along(x_high, "gx", 1)
    corners = [x_low[40:], x_high[40:]]
    y_low = passed_along(jnp.concatenate([y_low] + corners, 0), "gy", -1)
    y_high = passed_along(jnp.concatenate([y_high] + corners, 0), "gy", 1)

    (force,) = call(
        near_kernel,
        [SM] * 3 + [VM, HBM],
        [(VM, (2 * LANES, LANES), F32)],
        [
            (words.shape, I32),
            (),
            ((TARGET_ROWS * LANES, LANES), F32),
            ((40 * LANES, LANES), F32),
            ((32 * (tiles + 1), LANES), F32),
        ],
        "near",
        flops=10**9,
        moved=10**8,
    )(near_tile, near_source, counts, record, words)
    speeds, offsets = call(
        far_kernel,
        [SM] * 3 + [VM, HBM] + [VM] * 5,
        [(VM, (2 * LANES, LANES), F32)] * 2,
        [
            (words.shape, I32),
            (),
            ((2 * LANES, LANES), F32),
            ((TARGET_ROWS * LANES, LANES), F32),
            ((40 * 40, LANES), F32),
            ((32 * (tiles + 1), LANES), F32),
        ],
        "far",
    )(far_tile, far_source, counts, record, words, force, x_low, x_high, y_low, y_high)
    return unpair_rows(speeds), unpair_rows(offsets)


def solution(mesh):
    placed = (
        P(None, ("gx", "gy")),
        P(None, ("gx", "gy")),
        P(None, ("gx", "gy")),
        P(("gx", "gy")),
        P(("gx", "gy")),
        P(("gx", "gy")),
        P(("gx", "gy")),
        P(("gx", "gy")),
        P(None, ("gx", "gy")),
        P(None, ("gx", "gy")),
        P(("gx", "gy")),
        P(("gx", "gy"), None),
    )
    return jax.shard_map(
        body,
        mesh=mesh,
        in_specs=placed,
        out_specs=(P(None, ("gx", "gy")), P(None, ("gx", "gy"))),
        check_vma=False,
    )
```

```python
import functools

import jax
import jax.numpy as jnp
from jax import lax
from jax.experimental import pallas as pl
from jax.experimental.pallas import tpu as pltpu
from jax.sharding import PartitionSpec as P

F32 = jnp.float32
BF16 = jnp.bfloat16
I32 = jnp.int32

LANES = 128
PER_BLOCK = 3
NEAR_FLOOR = 0.5
BOND_COEFFICIENT = 0.005
SHIFT_STEP_SIZE = 0.5

PARTS = 3
MOVED_PARTS = (3, 3, 3, 3, 2, 2, 2, 2, 2)
SEND_ROWS = 24
SLOTS = 256
UNROLL = 4
TARGET_ROWS = 72
MIB = 1024 * 1024


def passed_along(block, axis, distance):
    devices = range(lax.axis_size(axis))
    route = [(i - distance, i) for i in devices if i - distance in devices]
    return lax.ppermute(block, axis, route)


def split(x, count=PARTS):
    parts = []
    for _ in range(count):
        part = x.astype(BF16)
        parts.append(part)
        x = x - part.astype(F32)
    return parts


def first_part(c):
    return sum(MOVED_PARTS[:c])


def added_parts(total, c, rows):
    at = first_part(c) * rows
    value = total[at : at + rows, :]
    for s in range(1, MOVED_PARTS[c]):
        value = value + total[at + s * rows : at + (s + 1) * rows, :]
    return value


def copied(pairs, sem):
    copies = [pltpu.make_async_copy(a, b, sem.at[i]) for i, (a, b) in enumerate(pairs)]
    for copy in copies:
        copy.start()
    return copies


def iota(shape, dim):
    return lax.broadcasted_iota(I32, shape, dim)


def ones_where(mask):
    return jnp.where(mask, 1.0, 0.0).astype(BF16)


def lookup_table(table, comp, x):
    turned = x.T
    turned = jnp.concatenate([turned[:64], turned[64:]], 1)
    for s, part in enumerate(split(turned, table.shape[1] // 256)):
        table[comp * 64 : (comp + 1) * 64, s * 256 : (s + 1) * 256] = part


def looked_up(tables, index):
    width = index.shape[1]
    high = ones_where(iota((256, width), 0) == ((index >> 7) + ((index & 64) << 1)))
    low = iota((64, width), 0) == (index & 63)
    values = []
    for table in tables:
        parts = table.shape[1] // 256
        found = jnp.dot(
            table[...], jnp.concatenate([high] * parts, 0), preferred_element_type=F32
        )
        for c in range(table.shape[0] // 64):
            chosen = jnp.where(low, found[c * 64 : (c + 1) * 64], 0.0)
            values.append(jnp.sum(chosen, axis=0, keepdims=True))
    return values


def two_rows(ref, first):
    return jnp.concatenate([ref[pl.ds(first, 1), :], ref[pl.ds(first + 1, 1), :]], 1)


NT = (((1,), (1,)), ((), ()))


def send_kernel(*refs):
    arguments, refs = refs[:9], refs[9:]
    (out, near_tile, near_source, far_tile, far_source, counts), refs = refs[:6], refs[6:]
    held, (sem, table, coarse, spread, place, total) = refs[:9], refs[9:]
    copies = copied(zip(arguments, held), sem)
    source, pos, dis, vel, sti, den, rows, slots, news = held
    for copy in copies:
        copy.wait()
    for c, ref in enumerate((pos, dis)):
        for d in range(2):
            lookup_table(table, 2 * c + d, ref[pl.ds(d, LANES, stride=2), :])
    for d in range(2):
        lookup_table(coarse, d, vel[pl.ds(d, LANES, stride=2), :])
    lookup_table(coarse, 2, sti[...])
    lookup_table(coarse, 3, den[...])
    total[...] = jnp.zeros_like(total)
    owners = out.shape[0] // SEND_ROWS
    tiles = source.shape[0]
    batch = place.shape[1] // SLOTS
    steps = rows.shape[0] // 2 // batch

    def step(k, carry):
        near, far = carry
        for i in range(tiles // steps):
            tile = k * (tiles // steps) + i
            src = source[tile]
            near_tile[near] = tile
            near_source[near] = src
            far_tile[far] = tile
            far_source[far] = src
            is_near = (src < LANES).astype(I32)
            near, far = near + is_near, far + 1 - is_near
        for i in range(batch):
            first = 2 * (k * batch + i)
            at_lanes = slice(i * SLOTS, (i + 1) * SLOTS)
            index = two_rows(rows, first)
            slot = two_rows(slots, first)
            new = two_rows(news, first)
            values = looked_up((table, coarse), index)
            values.append((new + 1).astype(F32))
            here = iota((owners, SLOTS), 0) == (slot >> 8)
            for c, value in enumerate(values):
                for s, part in enumerate(split(value, MOVED_PARTS[c])):
                    at = (first_part(c) + s) * owners
                    spread[at : at + owners, at_lanes] = jnp.where(
                        here, part.astype(F32), 0.0
                    ).astype(BF16)
            place[:, at_lanes] = ones_where(iota((SLOTS, SLOTS), 0) == (slot & 255))
        total[...] += lax.dot_general(spread[...], place[...], NT, preferred_element_type=F32)
        return near, far

    near, far = lax.fori_loop(0, steps, step, (jnp.int32(0), jnp.int32(0)))
    for i in range(UNROLL):
        near_tile[near + i] = tiles
        near_source[near + i] = 0
        far_tile[far + i] = tiles
        far_source[far + i] = LANES
    counts[0] = (near + UNROLL - 1) // UNROLL
    counts[1] = (far + UNROLL - 1) // UNROLL

    out[...] = jnp.zeros_like(out)
    for c in range(9):
        value = added_parts(total, c, owners)
        out[pl.ds(2 * c, owners, stride=SEND_ROWS), :] = value[:, :LANES]
        out[pl.ds(2 * c + 1, owners, stride=SEND_ROWS), :] = value[:, LANES:]


def receive_kernel(got, *refs):
    arguments, refs = refs[:7], refs[7:]
    (record, table, x_low, x_high), refs = refs[:4], refs[4:]
    held, (sem, spread, place, total) = refs[:7], refs[7:]
    copies = copied(zip(arguments, held), sem)
    pos, dis, vel, sti, den, edge_rows, corner_rows = held
    owners = got.shape[0] // SEND_ROWS
    batch = place.shape[1] // SLOTS
    total[...] = jnp.zeros_like(total)

    @pl.loop(0, owners // batch)
    def _(k):
        for i in range(batch):
            first = (k * batch + i) * SEND_ROWS
            at_lanes = slice(i * SLOTS, (i + 1) * SLOTS)
            row = two_rows(got, first + 16).astype(I32) - 1
            here = iota((64, SLOTS), 0) == (row >> 8)
            for c in range(8):
                value = two_rows(got, first + 2 * c)
                for s, part in enumerate(split(value, MOVED_PARTS[c])):
                    at = (first_part(c) + s) * 64
                    spread[at : at + 64, at_lanes] = jnp.where(
                        here, part.astype(F32), 0.0
                    ).astype(BF16)
            place[:, at_lanes] = ones_where(iota((256, SLOTS), 0) == (row & 255))
        total[...] += lax.dot_general(spread[...], place[...], NT, preferred_element_type=F32)

    for copy in copies:
        copy.wait()
    moved = added_parts(total, 6, 64) > 0.25
    for c in range(8):
        value = added_parts(total, c, 64)
        for half in range(2):
            if c < 6:
                ref = (pos, dis, vel)[c // 2]
                kept = ref[pl.ds(2 * half + c % 2, 64, stride=4), :]
            else:
                kept = (sti, den)[c - 6][pl.ds(half, 64, stride=2), :]
            lanes = slice(half * LANES, (half + 1) * LANES)
            chosen = jnp.where(moved[:, lanes], value[:, lanes], kept)
            if c == 6:
                chosen = jnp.sqrt(chosen)
            record[pl.ds(c * LANES + half, 64, stride=2), :] = chosen
    for c, source in enumerate((0, 1, 2, 3, 6)):
        lookup_table(table, c, record[source * LANES : (source + 1) * LANES, :])
    look_up_edges(table, edge_rows, ((0, x_low), (3, x_high)))
    corners = corner_rows[...]
    index = jnp.concatenate([corners[i : i + 1, :] for i in range(4)], 1)
    for ref in (x_low, x_high):
        ref[40:48, :] = jnp.zeros((8, LANES), F32)
    for c, value in enumerate(looked_up((table,), index)):
        x_low[40 + c : 41 + c, :] = value[:, :LANES]
        x_high[40 + c : 41 + c, :] = value[:, LANES:]


def look_up_edges(table, edge_rows, bundles):
    half = edge_rows.shape[1] // 512

    @pl.loop(0, half)
    def _(q):
        for edge, bundle in bundles:
            for i in range(2):
                at = q + i * half
                index = edge_rows[edge : edge + 1, pl.ds(pl.multiple_of(at * 256, 256), 256)]
                for c, value in enumerate(looked_up((table,), index)):
                    bundle[pl.ds(c * 8 + 2 * at, 1), :] = value[:, :LANES]
                    bundle[pl.ds(c * 8 + 2 * at + 1, 1), :] = value[:, LANES:]


def expand_kernel(record, table, rows, y_low, y_high, targets, sources, edge_rows, sem):
    copies = copied([(rows, edge_rows)], sem)
    expand_targets(record, targets)
    expand_sources(
        [record[c * LANES : (c + 1) * LANES, :] for c in (0, 1, 2, 3, 6)], sources
    )
    copies[0].wait()
    look_up_edges(table, edge_rows, ((1, y_low), (2, y_high)))


def expand_targets(record, targets):
    parts = [
        jnp.concatenate(split(record[c * LANES : (c + 1) * LANES, :]), 1) for c in range(4)
    ]
    values = jnp.concatenate(parts, 0)
    for r in range(0, 16, 2):
        shape = (LANES, 2 * LANES)
        lane = iota(shape, 1)
        chosen = ones_where(iota(shape, 0) == 8 * r + lane // 16)
        spread = jnp.dot(
            values, jnp.concatenate([chosen] * PARTS, 0), preferred_element_type=F32
        )
        for c in range(4):
            for half in range(2):
                targets[pl.ds(c * 16 + r + half, LANES, stride=TARGET_ROWS), :] = spread[
                    c * LANES : (c + 1) * LANES, half * LANES : (half + 1) * LANES
                ]


def expand_sources(arrays, sources):
    count = arrays[0].shape[0]
    values = jnp.concatenate([jnp.concatenate(split(a), 1) for a in arrays], 0)
    for b in range(0, 8, 2):
        shape = (LANES, 2 * LANES)
        lane = iota(shape, 1)
        chosen = ones_where(iota(shape, 0) == 8 * (lane % 16) + b + lane // LANES)
        spread = jnp.dot(
            values, jnp.concatenate([chosen] * PARTS, 0), preferred_element_type=F32
        )
        for c in range(5):
            for half in range(2):
                value = spread[c * count : (c + 1) * count, half * LANES : (half + 1) * LANES]
                if c == 4:
                    value = value * (2.0 ** -(b + half))
                sources[pl.ds(c * 8 + b + half, count, stride=40), :] = value


def tile_loop(steps, tile_ids, tile_sources, first_block, words, targets, sources, pushed):
    tiles = words.shape[0] // 16

    def one_tile(position):
        tile = tile_ids[position]
        base = (tile_sources[position] - first_block) * 40
        known = jnp.minimum(tile, tiles - 1)
        word = words[pl.ds((known >> 3) * LANES + (known & 7), 16, stride=8), :]
        block = pl.multiple_of(((known * 43691) >> 17) * TARGET_ROWS, 8)
        tx, ty, tu, tv = (targets[pl.ds(block + 16 * c, 16), :] for c in range(4))
        push_x = push_y = None
        for b in range(8):
            sx, sy, su, sv, root = (
                sources[pl.ds(base + 8 * c + b, 1), :] for c in range(5)
            )
            sep_x, sep_y = sx - tx, sy - ty
            rel_x, rel_y = su - tu, sv - tv
            square = sep_x * sep_x + sep_y * sep_y
            inverse = lax.rsqrt(jnp.maximum(square, NEAR_FLOOR * NEAR_FLOOR))
            intact = (word & (1 << b)).astype(F32)
            weight = (
                (sep_x * rel_x + sep_y * rel_y)
                * (inverse * inverse)
                * (inverse * root)
                * intact
            )
            more_x, more_y = weight * sep_x, weight * sep_y
            push_x = more_x if b == 0 else push_x + more_x
            push_y = more_y if b == 0 else push_y + more_y
        return tile, push_x, push_y

    @pl.loop(0, steps)
    def _(step):
        for tile, push_x, push_y in [one_tile(step * UNROLL + i) for i in range(UNROLL)]:
            at = pl.multiple_of(tile * 32, 32)
            pushed[pl.ds(at, 16), :] = push_x
            pushed[pl.ds(at + 16, 16), :] = push_y


def gather_force(pushed, force):
    many = 64
    shape = (LANES, LANES)
    chosen = ones_where(iota(shape, 0) // 16 == iota(shape, 1) % 8)
    chosen = jnp.concatenate([chosen] * 2, 0)
    own = iota((16, LANES), 1) // 8 == iota((16, LANES), 0)

    @pl.loop(0, force.shape[0] // 2 // many)
    def _(group):
        values = []
        for i in range(many):
            at = pl.multiple_of((group * many + i) * 32 * PER_BLOCK, 32)
            value = pushed[pl.ds(at, 32), :]
            for k in range(1, PER_BLOCK):
                value = value + pushed[pl.ds(at + 32 * k, 32), :]
            values.append(jnp.concatenate(split(value, 2), 1))
        sums = jnp.dot(jnp.concatenate(values, 0), chosen, preferred_element_type=F32)
        sums = jnp.where(own[None], sums.reshape(2 * many, 16, LANES), 0.0)
        force[pl.ds(pl.multiple_of(group * 2 * many, 2 * many), 2 * many), :] = jnp.sum(sums, axis=1)


def near_kernel(
    tile_ids, tile_sources, counts, targets, sources, words, force, pushed
):
    pushed[...] = jnp.zeros_like(pushed)
    tile_loop(counts[0], tile_ids, tile_sources, 0, words, targets, sources, pushed)
    gather_force(pushed, force)


def far_kernel(
    tile_ids, tile_sources, counts, record, targets, words, force,
    x_low, x_high, y_low, y_high, speeds, offsets, more, sources, pushed
):
    pushed[...] = jnp.zeros_like(pushed)
    halo = []
    left = iota((1, LANES), 1) < 64
    for c in range(5):
        edges = [ref[8 * c : 8 * c + 8, :] for ref in (x_low, y_low, y_high, x_high)]
        corners = [
            jnp.where(left, y_low[r + c : r + c + 1, :], y_high[r + c : r + c + 1, :])
            for r in (40, 48)
        ]
        halo.append(jnp.concatenate(edges + corners + [jnp.zeros((6, LANES), F32)], 0))
    expand_sources(halo, sources)
    tile_loop(counts[1], tile_ids, tile_sources, LANES, words, targets, sources, pushed)
    gather_force(pushed, more)
    root = record[6 * LANES : 7 * LANES, :]
    density = record[7 * LANES : 8 * LANES, :]
    for d in range(2):
        at = pl.ds(d, LANES, stride=2)
        total = force[at, :] + more[at, :]
        speed = record[(4 + d) * LANES : (5 + d) * LANES, :] + (
            BOND_COEFFICIENT * (total * root) / density
        )
        speeds[at, :] = speed
        offsets[at, :] = (
            record[(2 + d) * LANES : (3 + d) * LANES, :] + SHIFT_STEP_SIZE * speed
        )


VM = pl.BlockSpec(memory_space=pltpu.VMEM)
SM = pl.BlockSpec(memory_space=pltpu.SMEM)
HBM = pl.BlockSpec(memory_space=pltpu.HBM)


def call(kernel, in_specs, outs, scratch, name, vmem, flops=0, moved=0):
    return pl.pallas_call(
        kernel,
        name=name,
        in_specs=in_specs,
        out_specs=[spec for spec, _, _ in outs],
        out_shape=[jax.ShapeDtypeStruct(shape, dtype) for _, shape, dtype in outs],
        scratch_shapes=[
            pltpu.SemaphoreType.DMA(entry)
            if len(entry) == 1
            else (entry[2] if len(entry) == 3 else pltpu.VMEM)(*entry[:2])
            for entry in scratch
        ],
        cost_estimate=pl.CostEstimate(flops=flops, bytes_accessed=moved, transcendentals=0),
        compiler_params=pltpu.CompilerParams(vmem_limit_bytes=vmem * MIB),
    )


def pair_rows(x):
    return x.reshape(2, LANES, LANES).transpose(1, 0, 2).reshape(2 * LANES, LANES)


def unpair_rows(x):
    return x.reshape(LANES, 2, LANES).transpose(1, 0, 2).reshape(2, LANES * LANES)


def body(
    positions,
    displacement,
    velocity,
    stiffness,
    density,
    move_rows,
    move_slot,
    move_new,
    edge_rows,
    corner_rows,
    tile_src,
    bond_bits,
):
    owners = lax.axis_size("gy")
    tiles = tile_src.shape[0]
    state = (
        pair_rows(positions),
        pair_rows(displacement),
        pair_rows(velocity),
        stiffness.reshape(LANES, LANES),
        density.reshape(LANES, LANES),
    )
    moves = tuple(m.reshape(-1, LANES) for m in (move_rows, move_slot, move_new))
    words = (
        bond_bits.reshape(tiles // 8, 8, 16, LANES).transpose(0, 2, 1, 3).reshape(-1, LANES)
    )
    state, moves, (edge_rows, corner_rows, tile_src) = (
        tuple(pltpu.with_memory_space_constraint(x, pltpu.HBM) for x in group)
        for group in (state, moves, (edge_rows, corner_rows, tile_src))
    )

    batch = 4
    listed = tiles + UNROLL
    moved_parts = first_part(9)
    held = [((2 * LANES, LANES), F32)] * 3 + [((LANES, LANES), F32)] * 2
    outgoing, near_tile, near_source, far_tile, far_source, counts = call(
        send_kernel,
        [HBM] * 9,
        [(VM, (owners * SEND_ROWS, LANES), F32)]
        + [(SM, (listed,), I32)] * 4
        + [(SM, (2,), I32)],
        [(tile_src.shape, I32, pltpu.SMEM)]
        + held
        + [(moves[0].shape, I32)] * 3
        + [
            (9,),
            ((4 * 64, 3 * 256), BF16),
            ((4 * 64, 2 * 256), BF16),
            ((moved_parts * owners, batch * SLOTS), BF16),
            ((SLOTS, batch * SLOTS), BF16),
            ((moved_parts * owners, SLOTS), F32),
        ],
        "send",
        16,
    )(tile_src, *state, *moves)
    got = lax.all_to_all(
        outgoing.reshape(owners, SEND_ROWS, LANES), "gy", split_axis=0, concat_axis=0, tiled=True
    ).reshape(owners * SEND_ROWS, LANES)

    state_parts = first_part(8)
    record, table, x_low, x_high = call(
        receive_kernel,
        [VM] + [HBM] * 7,
        [(VM, (8 * LANES, LANES), F32), (VM, (5 * 64, PARTS * 256), BF16)]
        + [(VM, (48, LANES), F32)] * 2,
        held
        + [
            (edge_rows.shape, I32),
            (corner_rows.shape, I32),
            (7,),
            ((state_parts * 64, batch * SLOTS), BF16),
            ((256, batch * SLOTS), BF16),
            ((state_parts * 64, 256), F32),
        ],
        "receive",
        16,
    )(got, *state, edge_rows, corner_rows)

    x_low = passed_along(x_low, "gx", -1)
    x_high = passed_along(x_high, "gx", 1)
    y_low, y_high, targets, sources = call(
        expand_kernel,
        [VM, VM, HBM],
        [(VM, (40, LANES), F32)] * 2
        + [(VM, (TARGET_ROWS * LANES, LANES), F32), (VM, (40 * LANES, LANES), F32)],
        [(edge_rows.shape, I32), (1,)],
        "expand",
        8,
        flops=4 * 10**9,
        moved=10**7,
    )(record, table, edge_rows)
    corners = [x_low[40:], x_high[40:]]
    y_low = passed_along(jnp.concatenate([y_low] + corners, 0), "gy", -1)
    y_high = passed_along(jnp.concatenate([y_high] + corners, 0), "gy", 1)

    pushed = ((32 * (tiles + 1), LANES), F32)
    (force,) = call(
        near_kernel,
        [SM] * 3 + [VM] * 3,
        [(VM, (2 * LANES, LANES), F32)],
        [pushed],
        "near",
        12,
        flops=10**10,
        moved=10**7,
    )(near_tile, near_source, counts, targets, sources, words)
    speeds, offsets = call(
        far_kernel,
        [SM] * 3 + [VM] * 8,
        [(VM, (2 * LANES, LANES), F32)] * 2,
        [
            ((2 * LANES, LANES), F32),
            ((40 * 40, LANES), F32),
            pushed,
        ],
        "far",
        12,
    )(
        far_tile, far_source, counts, record, targets, words, force,
        x_low, x_high, y_low, y_high,
    )
    return unpair_rows(speeds), unpair_rows(offsets)


def solution(mesh):
    placed = (
        P(None, ("gx", "gy")),
        P(None, ("gx", "gy")),
        P(None, ("gx", "gy")),
        P(("gx", "gy")),
        P(("gx", "gy")),
        P(("gx", "gy")),
        P(("gx", "gy")),
        P(("gx", "gy")),
        P(None, ("gx", "gy")),
        P(None, ("gx", "gy")),
        P(("gx", "gy")),
        P(("gx", "gy"), None),
    )
    return jax.shard_map(
        body,
        mesh=mesh,
        in_specs=placed,
        out_specs=(P(None, ("gx", "gy")), P(None, ("gx", "gy"))),
        check_vma=False,
    )
```

```python
import functools

import jax
import jax.numpy as jnp
from jax import lax
from jax.experimental import pallas as pl
from jax.experimental.pallas import tpu as pltpu
from jax.sharding import PartitionSpec as P

F32 = jnp.float32
BF16 = jnp.bfloat16
I32 = jnp.int32

LANES = 128
PER_BLOCK = 3
NEAR_FLOOR = 0.5
BOND_COEFFICIENT = 0.005
SHIFT_STEP_SIZE = 0.5

PARTS = 3
MOVED_PARTS = (3, 3, 3, 3, 2, 2, 2, 2, 2)
SEND_ROWS = 24
SLOTS = 256
UNROLL = 8
TARGET_ROWS = 72
MIB = 1024 * 1024


def passed_along(block, axis, distance):
    devices = range(lax.axis_size(axis))
    route = [(i - distance, i) for i in devices if i - distance in devices]
    return lax.ppermute(block, axis, route)


def split(x, count=PARTS):
    parts = []
    for _ in range(count):
        part = x.astype(BF16)
        parts.append(part)
        x = x - part.astype(F32)
    return parts


def first_part(c):
    return sum(MOVED_PARTS[:c])


def added_parts(total, c, rows):
    at = first_part(c) * rows
    value = total[at : at + rows, :]
    for s in range(1, MOVED_PARTS[c]):
        value = value + total[at + s * rows : at + (s + 1) * rows, :]
    return value


def copied(pairs, sem):
    copies = [pltpu.make_async_copy(a, b, sem.at[i]) for i, (a, b) in enumerate(pairs)]
    for copy in copies:
        copy.start()
    return copies


def iota(shape, dim):
    return lax.broadcasted_iota(I32, shape, dim)


def ones_where(mask):
    return jnp.where(mask, 1.0, 0.0).astype(BF16)


def lookup_table(table, comp, x):
    turned = x.T
    turned = jnp.concatenate([turned[:64], turned[64:]], 1)
    for s, part in enumerate(split(turned, table.shape[1] // 256)):
        table[comp * 64 : (comp + 1) * 64, s * 256 : (s + 1) * 256] = part


def looked_up(tables, index):
    width = index.shape[1]
    high = ones_where(iota((256, width), 0) == ((index >> 7) + ((index & 64) << 1)))
    low = iota((64, width), 0) == (index & 63)
    values = []
    for table in tables:
        parts = table.shape[1] // 256
        found = jnp.dot(
            table[...], jnp.concatenate([high] * parts, 0), preferred_element_type=F32
        )
        for c in range(table.shape[0] // 64):
            chosen = jnp.where(low, found[c * 64 : (c + 1) * 64], 0.0)
            values.append(jnp.sum(chosen, axis=0, keepdims=True))
    return values


def two_rows(ref, first):
    return jnp.concatenate([ref[pl.ds(first, 1), :], ref[pl.ds(first + 1, 1), :]], 1)


NT = (((1,), (1,)), ((), ()))


def send_kernel(*refs):
    arguments, refs = refs[:9], refs[9:]
    (out, near_tile, near_source, far_tile, far_source, counts), refs = refs[:6], refs[6:]
    held, (sem, table, coarse, spread, place, total) = refs[:9], refs[9:]
    copies = copied(zip(arguments, held), sem)
    source, pos, dis, vel, sti, den, rows, slots, news = held
    for c, ref in enumerate((pos, dis)):
        copies[1 + c].wait()
        for d in range(2):
            lookup_table(table, 2 * c + d, ref[pl.ds(d, LANES, stride=2), :])
    copies[3].wait()
    for d in range(2):
        lookup_table(coarse, d, vel[pl.ds(d, LANES, stride=2), :])
    for c, ref in enumerate((sti, den)):
        copies[4 + c].wait()
        lookup_table(coarse, 2 + c, ref[...])
    for copy in copies[:1] + copies[6:]:
        copy.wait()
    total[...] = jnp.zeros_like(total)
    owners = out.shape[0] // SEND_ROWS
    tiles = source.shape[0]
    batch = place.shape[1] // SLOTS
    steps = rows.shape[0] // 2 // batch

    def step(k, carry):
        near, far = carry
        for i in range(tiles // steps):
            tile = k * (tiles // steps) + i
            src = source[tile]
            near_tile[near] = tile
            near_source[near] = src
            far_tile[far] = tile
            far_source[far] = src
            is_near = (src < LANES).astype(I32)
            near, far = near + is_near, far + 1 - is_near
        for i in range(batch):
            first = 2 * (k * batch + i)
            at_lanes = slice(i * SLOTS, (i + 1) * SLOTS)
            index = two_rows(rows, first)
            slot = two_rows(slots, first)
            new = two_rows(news, first)
            values = looked_up((table, coarse), index)
            values.append((new + 1).astype(F32))
            here = iota((owners, SLOTS), 0) == (slot >> 8)
            for c, value in enumerate(values):
                for s, part in enumerate(split(value, MOVED_PARTS[c])):
                    at = (first_part(c) + s) * owners
                    spread[at : at + owners, at_lanes] = jnp.where(
                        here, part.astype(F32), 0.0
                    ).astype(BF16)
            place[:, at_lanes] = ones_where(iota((SLOTS, SLOTS), 0) == (slot & 255))
        total[...] += lax.dot_general(spread[...], place[...], NT, preferred_element_type=F32)
        return near, far

    near, far = lax.fori_loop(0, steps, step, (jnp.int32(0), jnp.int32(0)))
    for i in range(UNROLL):
        near_tile[near + i] = tiles
        near_source[near + i] = 0
        far_tile[far + i] = tiles
        far_source[far + i] = LANES
    counts[0] = (near + UNROLL - 1) // UNROLL
    counts[1] = (far + UNROLL - 1) // UNROLL

    out[...] = jnp.zeros_like(out)
    for c in range(9):
        value = added_parts(total, c, owners)
        out[pl.ds(2 * c, owners, stride=SEND_ROWS), :] = value[:, :LANES]
        out[pl.ds(2 * c + 1, owners, stride=SEND_ROWS), :] = value[:, LANES:]


def receive_kernel(got, *refs):
    arguments, refs = refs[:7], refs[7:]
    (record, table, x_low, x_high), refs = refs[:4], refs[4:]
    held, (sem, spread, place, total) = refs[:7], refs[7:]
    copies = copied(zip(arguments, held), sem)
    pos, dis, vel, sti, den, edge_rows, corner_rows = held
    owners = got.shape[0] // SEND_ROWS
    batch = place.shape[1] // SLOTS
    total[...] = jnp.zeros_like(total)

    @pl.loop(0, owners // batch)
    def _(k):
        for i in range(batch):
            first = (k * batch + i) * SEND_ROWS
            at_lanes = slice(i * SLOTS, (i + 1) * SLOTS)
            row = two_rows(got, first + 16).astype(I32) - 1
            here = iota((64, SLOTS), 0) == (row >> 8)
            for c in range(8):
                value = two_rows(got, first + 2 * c)
                for s, part in enumerate(split(value, MOVED_PARTS[c])):
                    at = (first_part(c) + s) * 64
                    spread[at : at + 64, at_lanes] = jnp.where(
                        here, part.astype(F32), 0.0
                    ).astype(BF16)
            place[:, at_lanes] = ones_where(iota((256, SLOTS), 0) == (row & 255))
        total[...] += lax.dot_general(spread[...], place[...], NT, preferred_element_type=F32)

    for copy in copies:
        copy.wait()
    moved = added_parts(total, 6, 64) > 0.25
    for c in range(8):
        value = added_parts(total, c, 64)
        for half in range(2):
            if c < 6:
                ref = (pos, dis, vel)[c // 2]
                kept = ref[pl.ds(2 * half + c % 2, 64, stride=4), :]
            else:
                kept = (sti, den)[c - 6][pl.ds(half, 64, stride=2), :]
            lanes = slice(half * LANES, (half + 1) * LANES)
            chosen = jnp.where(moved[:, lanes], value[:, lanes], kept)
            if c == 6:
                chosen = jnp.sqrt(chosen)
            record[pl.ds(c * LANES + half, 64, stride=2), :] = chosen
    for c, source in enumerate((0, 1, 2, 3, 6)):
        lookup_table(table, c, record[source * LANES : (source + 1) * LANES, :])
    look_up_edges(table, edge_rows, ((0, x_low), (3, x_high)))
    corners = corner_rows[...]
    index = jnp.concatenate([corners[i : i + 1, :] for i in range(4)], 1)
    for ref in (x_low, x_high):
        ref[40:48, :] = jnp.zeros((8, LANES), F32)
    for c, value in enumerate(looked_up((table,), index)):
        x_low[40 + c : 41 + c, :] = value[:, :LANES]
        x_high[40 + c : 41 + c, :] = value[:, LANES:]


def look_up_edges(table, edge_rows, bundles):
    half = edge_rows.shape[1] // 512

    @pl.loop(0, half)
    def _(q):
        for edge, bundle in bundles:
            for i in range(2):
                at = q + i * half
                index = edge_rows[edge : edge + 1, pl.ds(pl.multiple_of(at * 256, 256), 256)]
                for c, value in enumerate(looked_up((table,), index)):
                    bundle[pl.ds(c * 8 + 2 * at, 1), :] = value[:, :LANES]
                    bundle[pl.ds(c * 8 + 2 * at + 1, 1), :] = value[:, LANES:]


def expand_kernel(record, table, rows, y_low, y_high, targets, sources, edge_rows, sem):
    copies = copied([(rows, edge_rows)], sem)
    expand_targets(record, targets)
    expand_sources(
        [record[c * LANES : (c + 1) * LANES, :] for c in (0, 1, 2, 3, 6)], sources
    )
    copies[0].wait()
    look_up_edges(table, edge_rows, ((1, y_low), (2, y_high)))


def expand_targets(record, targets):
    parts = [
        jnp.concatenate(split(record[c * LANES : (c + 1) * LANES, :]), 1) for c in range(4)
    ]
    values = jnp.concatenate(parts, 0)
    for r in range(0, 16, 2):
        shape = (LANES, 2 * LANES)
        lane = iota(shape, 1)
        chosen = ones_where(iota(shape, 0) == 8 * r + lane // 16)
        spread = jnp.dot(
            values, jnp.concatenate([chosen] * PARTS, 0), preferred_element_type=F32
        )
        for c in range(4):
            for half in range(2):
                targets[pl.ds(c * 16 + r + half, LANES, stride=TARGET_ROWS), :] = spread[
                    c * LANES : (c + 1) * LANES, half * LANES : (half + 1) * LANES
                ]


def expand_sources(arrays, sources):
    count = arrays[0].shape[0]
    values = jnp.concatenate([jnp.concatenate(split(a), 1) for a in arrays], 0)
    for b in range(0, 8, 2):
        shape = (LANES, 2 * LANES)
        lane = iota(shape, 1)
        chosen = ones_where(iota(shape, 0) == 8 * (lane % 16) + b + lane // LANES)
        spread = jnp.dot(
            values, jnp.concatenate([chosen] * PARTS, 0), preferred_element_type=F32
        )
        for c in range(5):
            for half in range(2):
                value = spread[c * count : (c + 1) * count, half * LANES : (half + 1) * LANES]
                if c == 4:
                    value = value * (2.0 ** -(b + half))
                sources[pl.ds(c * 8 + b + half, count, stride=40), :] = value


def tile_loop(steps, tile_ids, tile_sources, first_block, words, targets, sources, pushed):
    tiles = words.shape[0] // 16

    def one_tile(position):
        tile = tile_ids[position]
        base = (tile_sources[position] - first_block) * 40
        known = jnp.minimum(tile, tiles - 1)
        word = words[pl.ds((known >> 3) * LANES + (known & 7), 16, stride=8), :]
        block = pl.multiple_of(((known * 43691) >> 17) * TARGET_ROWS, 8)
        tx, ty, tu, tv = (targets[pl.ds(block + 16 * c, 16), :] for c in range(4))
        push_x = push_y = None
        for b in range(8):
            sx, sy, su, sv, root = (
                sources[pl.ds(base + 8 * c + b, 1), :] for c in range(5)
            )
            sep_x, sep_y = sx - tx, sy - ty
            rel_x, rel_y = su - tu, sv - tv
            square = sep_x * sep_x + sep_y * sep_y
            inverse = lax.rsqrt(jnp.maximum(square, NEAR_FLOOR * NEAR_FLOOR))
            intact = (word & (1 << b)).astype(F32)
            weight = (
                (sep_x * rel_x + sep_y * rel_y)
                * (inverse * inverse)
                * (inverse * root)
                * intact
            )
            more_x, more_y = weight * sep_x, weight * sep_y
            push_x = more_x if b == 0 else push_x + more_x
            push_y = more_y if b == 0 else push_y + more_y
        return tile, push_x, push_y

    @pl.loop(0, steps)
    def _(step):
        for tile, push_x, push_y in [one_tile(step * UNROLL + i) for i in range(UNROLL)]:
            at = pl.multiple_of(tile * 32, 32)
            pushed[pl.ds(at, 16), :] = push_x
            pushed[pl.ds(at + 16, 16), :] = push_y


def gather_force(pushed, further, force):
    many = 64
    shape = (LANES, LANES)
    chosen = ones_where(iota(shape, 0) // 16 == iota(shape, 1) % 8)
    chosen = jnp.concatenate([chosen] * 2, 0)
    own = iota((16, LANES), 1) // 8 == iota((16, LANES), 0)

    @pl.loop(0, force.shape[0] // 2 // many)
    def _(group):
        values = []
        for i in range(many):
            at = pl.multiple_of((group * many + i) * 32 * PER_BLOCK, 32)
            value = pushed[pl.ds(at, 32), :] + further[pl.ds(at, 32), :]
            for k in range(1, PER_BLOCK):
                tile = pl.ds(at + 32 * k, 32)
                value = value + (pushed[tile, :] + further[tile, :])
            values.append(jnp.concatenate(split(value, 2), 1))
        sums = jnp.dot(jnp.concatenate(values, 0), chosen, preferred_element_type=F32)
        sums = jnp.where(own[None], sums.reshape(2 * many, 16, LANES), 0.0)
        force[pl.ds(pl.multiple_of(group * 2 * many, 2 * many), 2 * many), :] = jnp.sum(sums, axis=1)


def near_kernel(
    tile_ids, tile_sources, counts, targets, sources, words, pushed
):
    pushed[...] = jnp.zeros_like(pushed)
    tile_loop(counts[0], tile_ids, tile_sources, 0, words, targets, sources, pushed)


def far_kernel(
    tile_ids, tile_sources, counts, record, targets, words, near_pushed,
    x_low, x_high, y_low, y_high, speeds, offsets, force, sources, pushed
):
    pushed[...] = jnp.zeros_like(pushed)
    halo = []
    left = iota((1, LANES), 1) < 64
    for c in range(5):
        edges = [ref[8 * c : 8 * c + 8, :] for ref in (x_low, y_low, y_high, x_high)]
        corners = [
            jnp.where(left, y_low[r + c : r + c + 1, :], y_high[r + c : r + c + 1, :])
            for r in (40, 48)
        ]
        halo.append(jnp.concatenate(edges + corners + [jnp.zeros((6, LANES), F32)], 0))
    expand_sources(halo, sources)
    tile_loop(counts[1], tile_ids, tile_sources, LANES, words, targets, sources, pushed)
    gather_force(near_pushed, pushed, force)
    root = record[6 * LANES : 7 * LANES, :]
    density = record[7 * LANES : 8 * LANES, :]
    for d in range(2):
        at = pl.ds(d, LANES, stride=2)
        total = force[at, :]
        speed = record[(4 + d) * LANES : (5 + d) * LANES, :] + (
            BOND_COEFFICIENT * (total * root) / density
        )
        speeds[at, :] = speed
        offsets[at, :] = (
            record[(2 + d) * LANES : (3 + d) * LANES, :] + SHIFT_STEP_SIZE * speed
        )


VM = pl.BlockSpec(memory_space=pltpu.VMEM)
SM = pl.BlockSpec(memory_space=pltpu.SMEM)
HBM = pl.BlockSpec(memory_space=pltpu.HBM)


def call(kernel, in_specs, outs, scratch, name, vmem, flops=0, moved=0):
    return pl.pallas_call(
        kernel,
        name=name,
        in_specs=in_specs,
        out_specs=[spec for spec, _, _ in outs],
        out_shape=[jax.ShapeDtypeStruct(shape, dtype) for _, shape, dtype in outs],
        scratch_shapes=[
            pltpu.SemaphoreType.DMA(entry)
            if len(entry) == 1
            else (entry[2] if len(entry) == 3 else pltpu.VMEM)(*entry[:2])
            for entry in scratch
        ],
        cost_estimate=pl.CostEstimate(flops=flops, bytes_accessed=moved, transcendentals=0),
        compiler_params=pltpu.CompilerParams(vmem_limit_bytes=vmem * MIB),
    )


def pair_rows(x):
    return x.reshape(2, LANES, LANES).transpose(1, 0, 2).reshape(2 * LANES, LANES)


def unpair_rows(x):
    return x.reshape(LANES, 2, LANES).transpose(1, 0, 2).reshape(2, LANES * LANES)


def body(
    positions,
    displacement,
    velocity,
    stiffness,
    density,
    move_rows,
    move_slot,
    move_new,
    edge_rows,
    corner_rows,
    tile_src,
    bond_bits,
):
    owners = lax.axis_size("gy")
    tiles = tile_src.shape[0]
    state = (
        pair_rows(positions),
        pair_rows(displacement),
        pair_rows(velocity),
        stiffness.reshape(LANES, LANES),
        density.reshape(LANES, LANES),
    )
    moves = tuple(m.reshape(-1, LANES) for m in (move_rows, move_slot, move_new))
    words = (
        bond_bits.reshape(tiles // 8, 8, 16, LANES).transpose(0, 2, 1, 3).reshape(-1, LANES)
    )
    state, moves, (edge_rows, corner_rows, tile_src) = (
        tuple(pltpu.with_memory_space_constraint(x, pltpu.HBM) for x in group)
        for group in (state, moves, (edge_rows, corner_rows, tile_src))
    )

    batch = 16
    listed = tiles + UNROLL
    moved_parts = first_part(9)
    held = [((2 * LANES, LANES), F32)] * 3 + [((LANES, LANES), F32)] * 2
    outgoing, near_tile, near_source, far_tile, far_source, counts = call(
        send_kernel,
        [HBM] * 9,
        [(VM, (owners * SEND_ROWS, LANES), F32)]
        + [(SM, (listed,), I32)] * 4
        + [(SM, (2,), I32)],
        [(tile_src.shape, I32, pltpu.SMEM)]
        + held
        + [(moves[0].shape, I32)] * 3
        + [
            (9,),
            ((4 * 64, 3 * 256), BF16),
            ((4 * 64, 2 * 256), BF16),
            ((moved_parts * owners, batch * SLOTS), BF16),
            ((SLOTS, batch * SLOTS), BF16),
            ((moved_parts * owners, SLOTS), F32),
        ],
        "send",
        24,
    )(tile_src, *state, *moves)
    got = lax.all_to_all(
        outgoing.reshape(owners, SEND_ROWS, LANES), "gy", split_axis=0, concat_axis=0, tiled=True
    ).reshape(owners * SEND_ROWS, LANES)

    state_parts = first_part(8)
    record, table, x_low, x_high = call(
        receive_kernel,
        [VM] + [HBM] * 7,
        [(VM, (8 * LANES, LANES), F32), (VM, (5 * 64, PARTS * 256), BF16)]
        + [(VM, (48, LANES), F32)] * 2,
        held
        + [
            (edge_rows.shape, I32),
            (corner_rows.shape, I32),
            (7,),
            ((state_parts * 64, batch * SLOTS), BF16),
            ((256, batch * SLOTS), BF16),
            ((state_parts * 64, 256), F32),
        ],
        "receive",
        24,
    )(got, *state, edge_rows, corner_rows)

    x_low = passed_along(x_low, "gx", -1)
    x_high = passed_along(x_high, "gx", 1)
    y_low, y_high, targets, sources = call(
        expand_kernel,
        [VM, VM, HBM],
        [(VM, (40, LANES), F32)] * 2
        + [(VM, (TARGET_ROWS * LANES, LANES), F32), (VM, (40 * LANES, LANES), F32)],
        [(edge_rows.shape, I32), (1,)],
        "expand",
        8,
        flops=4 * 10**9,
        moved=10**7,
    )(record, table, edge_rows)
    corners = [x_low[40:], x_high[40:]]
    y_low = passed_along(jnp.concatenate([y_low] + corners, 0), "gy", -1)
    y_high = passed_along(jnp.concatenate([y_high] + corners, 0), "gy", 1)

    pushed = ((32 * (tiles + 1), LANES), F32)
    (near_pushed,) = call(
        near_kernel,
        [SM] * 3 + [VM] * 3,
        [(VM, *pushed)],
        [],
        "near",
        8,
        flops=10**10,
        moved=10**7,
    )(near_tile, near_source, counts, targets, sources, words)
    speeds, offsets = call(
        far_kernel,
        [SM] * 3 + [VM] * 8,
        [(VM, (2 * LANES, LANES), F32)] * 2,
        [
            ((2 * LANES, LANES), F32),
            ((40 * 40, LANES), F32),
            pushed,
        ],
        "far",
        12,
    )(
        far_tile, far_source, counts, record, targets, words, near_pushed,
        x_low, x_high, y_low, y_high,
    )
    return unpair_rows(speeds), unpair_rows(offsets)


def solution(mesh):
    placed = (
        P(None, ("gx", "gy")),
        P(None, ("gx", "gy")),
        P(None, ("gx", "gy")),
        P(("gx", "gy")),
        P(("gx", "gy")),
        P(("gx", "gy")),
        P(("gx", "gy")),
        P(("gx", "gy")),
        P(None, ("gx", "gy")),
        P(None, ("gx", "gy")),
        P(("gx", "gy")),
        P(("gx", "gy"), None),
    )
    return jax.shard_map(
        body,
        mesh=mesh,
        in_specs=placed,
        out_specs=(P(None, ("gx", "gy")), P(None, ("gx", "gy"))),
        check_vma=False,
    )
```

```python
import functools

import jax
import jax.numpy as jnp
from jax import lax
from jax.experimental import pallas as pl
from jax.experimental.pallas import tpu as pltpu
from jax.sharding import PartitionSpec as P

F32 = jnp.float32
BF16 = jnp.bfloat16
I32 = jnp.int32

LANES = 128
PER_BLOCK = 3
NEAR_FLOOR = 0.5
BOND_COEFFICIENT = 0.005
SHIFT_STEP_SIZE = 0.5

PARTS = 3
MOVED_PARTS = (3, 3, 3, 3, 2, 2, 2, 2, 2)
SEND_ROWS = 24
SLOTS = 256
UNROLL = 8
TARGET_ROWS = 72
MIB = 1024 * 1024


def passed_along(block, axis, distance):
    devices = range(lax.axis_size(axis))
    route = [(i - distance, i) for i in devices if i - distance in devices]
    return lax.ppermute(block, axis, route)


def split(x, count=PARTS):
    parts = []
    for _ in range(count):
        part = x.astype(BF16)
        parts.append(part)
        x = x - part.astype(F32)
    return parts


def first_part(c):
    return sum(MOVED_PARTS[:c])


def added_parts(total, c, rows):
    at = first_part(c) * rows
    value = total[at : at + rows, :]
    for s in range(1, MOVED_PARTS[c]):
        value = value + total[at + s * rows : at + (s + 1) * rows, :]
    return value


def copied(pairs, sem):
    copies = [pltpu.make_async_copy(a, b, sem.at[i]) for i, (a, b) in enumerate(pairs)]
    for copy in copies:
        copy.start()
    return copies


def iota(shape, dim):
    return lax.broadcasted_iota(I32, shape, dim)


def ones_where(mask):
    return jnp.where(mask, 1.0, 0.0).astype(BF16)


def lookup_table(table, comp, x):
    turned = x.T
    turned = jnp.concatenate([turned[:64], turned[64:]], 1)
    for s, part in enumerate(split(turned, table.shape[1] // 256)):
        table[comp * 64 : (comp + 1) * 64, s * 256 : (s + 1) * 256] = part


def looked_up(tables, index):
    width = index.shape[1]
    high = ones_where(iota((256, width), 0) == ((index >> 7) + ((index & 64) << 1)))
    low = iota((64, width), 0) == (index & 63)
    values = []
    for table in tables:
        parts = table.shape[1] // 256
        found = jnp.dot(
            table[...], jnp.concatenate([high] * parts, 0), preferred_element_type=F32
        )
        for c in range(table.shape[0] // 64):
            chosen = jnp.where(low, found[c * 64 : (c + 1) * 64], 0.0)
            values.append(jnp.sum(chosen, axis=0, keepdims=True))
    return values


def two_rows(ref, first):
    return jnp.concatenate([ref[pl.ds(first, 1), :], ref[pl.ds(first + 1, 1), :]], 1)


NT = (((1,), (1,)), ((), ()))


def send_kernel(*refs):
    arguments, refs = refs[:9], refs[9:]
    (out, near_tile, near_source, far_tile, far_source, counts), refs = refs[:6], refs[6:]
    held, (sem, table, coarse, spread, place, total) = refs[:9], refs[9:]
    copies = copied(zip(arguments, held), sem)
    source, pos, dis, vel, sti, den, rows, slots, news = held
    for c, ref in enumerate((pos, dis)):
        copies[1 + c].wait()
        for d in range(2):
            lookup_table(table, 2 * c + d, ref[pl.ds(d, LANES, stride=2), :])
    copies[3].wait()
    for d in range(2):
        lookup_table(coarse, d, vel[pl.ds(d, LANES, stride=2), :])
    for c, ref in enumerate((sti, den)):
        copies[4 + c].wait()
        lookup_table(coarse, 2 + c, ref[...])
    for copy in copies[:1] + copies[6:]:
        copy.wait()
    total[...] = jnp.zeros_like(total)
    owners = out.shape[0] // SEND_ROWS
    tiles = source.shape[0]
    batch = place.shape[1] // SLOTS
    steps = rows.shape[0] // 2 // batch

    def step(k, carry):
        near, far = carry
        for i in range(tiles // steps):
            tile = k * (tiles // steps) + i
            src = source[tile]
            near_tile[near] = tile
            near_source[near] = src
            far_tile[far] = tile
            far_source[far] = src
            is_near = (src < LANES).astype(I32)
            near, far = near + is_near, far + 1 - is_near
        for i in range(batch):
            first = 2 * (k * batch + i)
            at_lanes = slice(i * SLOTS, (i + 1) * SLOTS)
            index = two_rows(rows, first)
            slot = two_rows(slots, first)
            new = two_rows(news, first)
            values = looked_up((table, coarse), index)
            values.append((new + 1).astype(F32))
            here = iota((owners, SLOTS), 0) == (slot >> 8)
            for c, value in enumerate(values):
                for s, part in enumerate(split(value, MOVED_PARTS[c])):
                    at = (first_part(c) + s) * owners
                    spread[at : at + owners, at_lanes] = jnp.where(
                        here, part.astype(F32), 0.0
                    ).astype(BF16)
            place[:, at_lanes] = ones_where(iota((SLOTS, SLOTS), 0) == (slot & 255))
        total[...] += lax.dot_general(spread[...], place[...], NT, preferred_element_type=F32)
        return near, far

    near, far = lax.fori_loop(0, steps, step, (jnp.int32(0), jnp.int32(0)))
    for i in range(UNROLL):
        near_tile[near + i] = tiles
        near_source[near + i] = 0
        far_tile[far + i] = tiles
        far_source[far + i] = LANES
    counts[0] = (near + UNROLL - 1) // UNROLL
    counts[1] = (far + UNROLL - 1) // UNROLL

    out[...] = jnp.zeros_like(out)
    for c in range(9):
        value = added_parts(total, c, owners)
        out[pl.ds(2 * c, owners, stride=SEND_ROWS), :] = value[:, :LANES]
        out[pl.ds(2 * c + 1, owners, stride=SEND_ROWS), :] = value[:, LANES:]


def receive_kernel(got, *refs):
    arguments, refs = refs[:7], refs[7:]
    (record, table, x_low, x_high), refs = refs[:4], refs[4:]
    held, (sem, spread, place, total) = refs[:7], refs[7:]
    copies = copied(zip(arguments, held), sem)
    pos, dis, vel, sti, den, edge_rows, corner_rows = held
    owners = got.shape[0] // SEND_ROWS
    batch = place.shape[1] // SLOTS
    total[...] = jnp.zeros_like(total)

    @pl.loop(0, owners // batch)
    def _(k):
        for i in range(batch):
            first = (k * batch + i) * SEND_ROWS
            at_lanes = slice(i * SLOTS, (i + 1) * SLOTS)
            row = two_rows(got, first + 16).astype(I32) - 1
            here = iota((64, SLOTS), 0) == (row >> 8)
            for c in range(8):
                value = two_rows(got, first + 2 * c)
                for s, part in enumerate(split(value, MOVED_PARTS[c])):
                    at = (first_part(c) + s) * 64
                    spread[at : at + 64, at_lanes] = jnp.where(
                        here, part.astype(F32), 0.0
                    ).astype(BF16)
            place[:, at_lanes] = ones_where(iota((256, SLOTS), 0) == (row & 255))
        total[...] += lax.dot_general(spread[...], place[...], NT, preferred_element_type=F32)

    for copy in copies:
        copy.wait()
    moved = added_parts(total, 6, 64) > 0.25
    for c in range(8):
        value = added_parts(total, c, 64)
        for half in range(2):
            if c < 6:
                ref = (pos, dis, vel)[c // 2]
                kept = ref[pl.ds(2 * half + c % 2, 64, stride=4), :]
            else:
                kept = (sti, den)[c - 6][pl.ds(half, 64, stride=2), :]
            lanes = slice(half * LANES, (half + 1) * LANES)
            chosen = jnp.where(moved[:, lanes], value[:, lanes], kept)
            if c == 6:
                chosen = jnp.sqrt(chosen)
            record[pl.ds(c * LANES + half, 64, stride=2), :] = chosen
    for c, source in enumerate((0, 1, 2, 3, 6)):
        lookup_table(table, c, record[source * LANES : (source + 1) * LANES, :])
    look_up_edges(table, edge_rows, ((0, x_low), (3, x_high)))
    corners = corner_rows[...]
    index = jnp.concatenate([corners[i : i + 1, :] for i in range(4)], 1)
    for ref in (x_low, x_high):
        ref[40:48, :] = jnp.zeros((8, LANES), F32)
    for c, value in enumerate(looked_up((table,), index)):
        x_low[40 + c : 41 + c, :] = value[:, :LANES]
        x_high[40 + c : 41 + c, :] = value[:, LANES:]


def look_up_edges(table, edge_rows, bundles):
    for edge, bundle in bundles:
        for at in range(edge_rows.shape[1] // 256):
            index = edge_rows[edge : edge + 1, at * 256 : (at + 1) * 256]
            for c, value in enumerate(looked_up((table,), index)):
                row = c * 8 + 2 * at
                bundle[row : row + 1, :] = value[:, :LANES]
                bundle[row + 1 : row + 2, :] = value[:, LANES:]


def expand_kernel(record, table, rows, y_low, y_high, targets, sources, edge_rows, sem):
    copies = copied([(rows, edge_rows)], sem)
    expand_targets(record, targets)
    expand_sources(
        [record[c * LANES : (c + 1) * LANES, :] for c in (0, 1, 2, 3, 6)], sources
    )
    copies[0].wait()
    look_up_edges(table, edge_rows, ((1, y_low), (2, y_high)))


def expand_targets(record, targets):
    parts = [
        jnp.concatenate(split(record[c * LANES : (c + 1) * LANES, :]), 1) for c in range(4)
    ]
    values = jnp.concatenate(parts, 0)
    for r in range(0, 16, 2):
        shape = (LANES, 2 * LANES)
        lane = iota(shape, 1)
        chosen = ones_where(iota(shape, 0) == 8 * r + lane // 16)
        spread = jnp.dot(
            values, jnp.concatenate([chosen] * PARTS, 0), preferred_element_type=F32
        )
        for c in range(4):
            for half in range(2):
                targets[pl.ds(c * 16 + r + half, LANES, stride=TARGET_ROWS), :] = spread[
                    c * LANES : (c + 1) * LANES, half * LANES : (half + 1) * LANES
                ]


def expand_sources(arrays, sources):
    count = arrays[0].shape[0]
    values = jnp.concatenate([jnp.concatenate(split(a), 1) for a in arrays], 0)
    for b in range(0, 8, 2):
        shape = (LANES, 2 * LANES)
        lane = iota(shape, 1)
        chosen = ones_where(iota(shape, 0) == 8 * (lane % 16) + b + lane // LANES)
        spread = jnp.dot(
            values, jnp.concatenate([chosen] * PARTS, 0), preferred_element_type=F32
        )
        for c in range(5):
            for half in range(2):
                value = spread[c * count : (c + 1) * count, half * LANES : (half + 1) * LANES]
                if c == 4:
                    value = value * (2.0 ** -(b + half))
                sources[pl.ds(c * 8 + b + half, count, stride=40), :] = value


def tile_loop(steps, tile_ids, tile_sources, first_block, words, targets, sources, pushed):
    tiles = words.shape[0] // 16

    def one_tile(position):
        tile = tile_ids[position]
        base = (tile_sources[position] - first_block) * 40
        known = jnp.minimum(tile, tiles - 1)
        word = words[pl.ds((known >> 3) * LANES + (known & 7), 16, stride=8), :]
        block = pl.multiple_of(((known * 43691) >> 17) * TARGET_ROWS, 8)
        tx, ty, tu, tv = (targets[pl.ds(block + 16 * c, 16), :] for c in range(4))
        push_x = push_y = None
        for b in range(8):
            sx, sy, su, sv, root = (
                sources[pl.ds(base + 8 * c + b, 1), :] for c in range(5)
            )
            sep_x, sep_y = sx - tx, sy - ty
            rel_x, rel_y = su - tu, sv - tv
            square = sep_x * sep_x + sep_y * sep_y
            inverse = lax.rsqrt(jnp.maximum(square, NEAR_FLOOR * NEAR_FLOOR))
            intact = (word & (1 << b)).astype(F32)
            weight = (
                (sep_x * rel_x + sep_y * rel_y)
                * (inverse * inverse)
                * (inverse * root)
                * intact
            )
            more_x, more_y = weight * sep_x, weight * sep_y
            push_x = more_x if b == 0 else push_x + more_x
            push_y = more_y if b == 0 else push_y + more_y
        return tile, push_x, push_y

    @pl.loop(0, steps)
    def _(step):
        for tile, push_x, push_y in [one_tile(step * UNROLL + i) for i in range(UNROLL)]:
            at = pl.multiple_of(tile * 32, 32)
            pushed[pl.ds(at, 16), :] = push_x
            pushed[pl.ds(at + 16, 16), :] = push_y


def gather_force(pushed, further, force):
    many = 64
    shape = (LANES, LANES)
    chosen = ones_where(iota(shape, 0) // 16 == iota(shape, 1) % 8)
    chosen = jnp.concatenate([chosen] * 2, 0)
    own = iota((16, LANES), 1) // 8 == iota((16, LANES), 0)

    @pl.loop(0, force.shape[0] // 2 // many)
    def _(group):
        values = []
        for i in range(many):
            at = pl.multiple_of((group * many + i) * 32 * PER_BLOCK, 32)
            value = pushed[pl.ds(at, 32), :] + further[pl.ds(at, 32), :]
            for k in range(1, PER_BLOCK):
                tile = pl.ds(at + 32 * k, 32)
                value = value + (pushed[tile, :] + further[tile, :])
            values.append(jnp.concatenate(split(value, 2), 1))
        sums = jnp.dot(jnp.concatenate(values, 0), chosen, preferred_element_type=F32)
        sums = jnp.where(own[None], sums.reshape(2 * many, 16, LANES), 0.0)
        force[pl.ds(pl.multiple_of(group * 2 * many, 2 * many), 2 * many), :] = jnp.sum(sums, axis=1)


def near_kernel(
    tile_ids, tile_sources, counts, targets, sources, words, pushed
):
    pushed[...] = jnp.zeros_like(pushed)
    tile_loop(counts[0], tile_ids, tile_sources, 0, words, targets, sources, pushed)


def far_kernel(
    tile_ids, tile_sources, counts, record, targets, words, near_pushed,
    x_low, x_high, y_low, y_high, speeds, offsets, force, sources, pushed
):
    pushed[...] = jnp.zeros_like(pushed)
    halo = []
    left = iota((1, LANES), 1) < 64
    for c in range(5):
        edges = [ref[8 * c : 8 * c + 8, :] for ref in (x_low, y_low, y_high, x_high)]
        corners = [
            jnp.where(left, y_low[r + c : r + c + 1, :], y_high[r + c : r + c + 1, :])
            for r in (40, 48)
        ]
        halo.append(jnp.concatenate(edges + corners + [jnp.zeros((6, LANES), F32)], 0))
    expand_sources(halo, sources)
    tile_loop(counts[1], tile_ids, tile_sources, LANES, words, targets, sources, pushed)
    gather_force(near_pushed, pushed, force)
    root = record[6 * LANES : 7 * LANES, :]
    density = record[7 * LANES : 8 * LANES, :]
    for d in range(2):
        at = pl.ds(d, LANES, stride=2)
        total = force[at, :]
        speed = record[(4 + d) * LANES : (5 + d) * LANES, :] + (
            BOND_COEFFICIENT * (total * root) / density
        )
        speeds[at, :] = speed
        offsets[at, :] = (
            record[(2 + d) * LANES : (3 + d) * LANES, :] + SHIFT_STEP_SIZE * speed
        )


VM = pl.BlockSpec(memory_space=pltpu.VMEM)
SM = pl.BlockSpec(memory_space=pltpu.SMEM)
HBM = pl.BlockSpec(memory_space=pltpu.HBM)


def call(kernel, in_specs, outs, scratch, name, vmem, flops=0, moved=0):
    return pl.pallas_call(
        kernel,
        name=name,
        in_specs=in_specs,
        out_specs=[spec for spec, _, _ in outs],
        out_shape=[jax.ShapeDtypeStruct(shape, dtype) for _, shape, dtype in outs],
        scratch_shapes=[
            pltpu.SemaphoreType.DMA(entry)
            if len(entry) == 1
            else (entry[2] if len(entry) == 3 else pltpu.VMEM)(*entry[:2])
            for entry in scratch
        ],
        cost_estimate=pl.CostEstimate(flops=flops, bytes_accessed=moved, transcendentals=0),
        compiler_params=pltpu.CompilerParams(vmem_limit_bytes=vmem * MIB),
    )


def pair_rows(x):
    return x.reshape(2, LANES, LANES).transpose(1, 0, 2).reshape(2 * LANES, LANES)


def unpair_rows(x):
    return x.reshape(LANES, 2, LANES).transpose(1, 0, 2).reshape(2, LANES * LANES)


def body(
    positions,
    displacement,
    velocity,
    stiffness,
    density,
    move_rows,
    move_slot,
    move_new,
    edge_rows,
    corner_rows,
    tile_src,
    bond_bits,
):
    owners = lax.axis_size("gy")
    tiles = tile_src.shape[0]
    state = (
        pair_rows(positions),
        pair_rows(displacement),
        pair_rows(velocity),
        stiffness.reshape(LANES, LANES),
        density.reshape(LANES, LANES),
    )
    moves = tuple(m.reshape(-1, LANES) for m in (move_rows, move_slot, move_new))
    words = (
        bond_bits.reshape(tiles // 8, 8, 16, LANES).transpose(0, 2, 1, 3).reshape(-1, LANES)
    )
    state, moves, (edge_rows, corner_rows, tile_src) = (
        tuple(pltpu.with_memory_space_constraint(x, pltpu.HBM) for x in group)
        for group in (state, moves, (edge_rows, corner_rows, tile_src))
    )

    batch = 16
    listed = tiles + UNROLL
    moved_parts = first_part(9)
    held = [((2 * LANES, LANES), F32)] * 3 + [((LANES, LANES), F32)] * 2
    outgoing, near_tile, near_source, far_tile, far_source, counts = call(
        send_kernel,
        [HBM] * 9,
        [(VM, (owners * SEND_ROWS, LANES), F32)]
        + [(SM, (listed,), I32)] * 4
        + [(SM, (2,), I32)],
        [(tile_src.shape, I32, pltpu.SMEM)]
        + held
        + [(moves[0].shape, I32)] * 3
        + [
            (9,),
            ((4 * 64, 3 * 256), BF16),
            ((4 * 64, 2 * 256), BF16),
            ((moved_parts * owners, batch * SLOTS), BF16),
            ((SLOTS, batch * SLOTS), BF16),
            ((moved_parts * owners, SLOTS), F32),
        ],
        "send",
        24,
    )(tile_src, *state, *moves)
    got = lax.all_to_all(
        outgoing.reshape(owners, SEND_ROWS, LANES), "gy", split_axis=0, concat_axis=0, tiled=True
    ).reshape(owners * SEND_ROWS, LANES)

    state_parts = first_part(8)
    record, table, x_low, x_high = call(
        receive_kernel,
        [VM] + [HBM] * 7,
        [(VM, (8 * LANES, LANES), F32), (VM, (5 * 64, PARTS * 256), BF16)]
        + [(VM, (48, LANES), F32)] * 2,
        held
        + [
            (edge_rows.shape, I32),
            (corner_rows.shape, I32),
            (7,),
            ((state_parts * 64, batch * SLOTS), BF16),
            ((256, batch * SLOTS), BF16),
            ((state_parts * 64, 256), F32),
        ],
        "receive",
        24,
    )(got, *state, edge_rows, corner_rows)

    x_low = passed_along(x_low, "gx", -1)
    x_high = passed_along(x_high, "gx", 1)
    y_low, y_high, targets, sources = call(
        expand_kernel,
        [VM, VM, HBM],
        [(VM, (40, LANES), F32)] * 2
        + [(VM, (TARGET_ROWS * LANES, LANES), F32), (VM, (40 * LANES, LANES), F32)],
        [(edge_rows.shape, I32), (1,)],
        "expand",
        8,
        flops=4 * 10**9,
        moved=10**7,
    )(record, table, edge_rows)
    corners = [x_low[40:], x_high[40:]]
    y_low = passed_along(jnp.concatenate([y_low] + corners, 0), "gy", -1)
    y_high = passed_along(jnp.concatenate([y_high] + corners, 0), "gy", 1)

    pushed = ((32 * (tiles + 1), LANES), F32)
    (near_pushed,) = call(
        near_kernel,
        [SM] * 3 + [VM] * 3,
        [(VM, *pushed)],
        [],
        "near",
        8,
        flops=10**10,
        moved=10**7,
    )(near_tile, near_source, counts, targets, sources, words)
    speeds, offsets = call(
        far_kernel,
        [SM] * 3 + [VM] * 8,
        [(VM, (2 * LANES, LANES), F32)] * 2,
        [
            ((2 * LANES, LANES), F32),
            ((40 * 40, LANES), F32),
            pushed,
        ],
        "far",
        12,
    )(
        far_tile, far_source, counts, record, targets, words, near_pushed,
        x_low, x_high, y_low, y_high,
    )
    return unpair_rows(speeds), unpair_rows(offsets)


def solution(mesh):
    placed = (
        P(None, ("gx", "gy")),
        P(None, ("gx", "gy")),
        P(None, ("gx", "gy")),
        P(("gx", "gy")),
        P(("gx", "gy")),
        P(("gx", "gy")),
        P(("gx", "gy")),
        P(("gx", "gy")),
        P(None, ("gx", "gy")),
        P(None, ("gx", "gy")),
        P(("gx", "gy")),
        P(("gx", "gy"), None),
    )
    return jax.shard_map(
        body,
        mesh=mesh,
        in_specs=placed,
        out_specs=(P(None, ("gx", "gy")), P(None, ("gx", "gy"))),
        check_vma=False,
    )
```
